32 devices in a mesh: groups: 2 (over y), seq: 4 (over z), head: 4 (over x, core).
Axes of the slice: x: 2, y: 2, z: 4, core: 2. Of those that a mesh axis runs over, the one named last changes fastest.
Arguments:
- segment_query: bfloat16 [512, 4096], P(('groups', 'seq'), 'head'), parts along dimension 0, may hold values from -8 to 8
- segment_memory: bfloat16 [512, 2, 1024], P(('groups', 'seq'), None, 'head'), parts along dimension 0, may hold values from -8 to 8
- finished_memory: bfloat16 [2048, 2, 1024], P(('groups', 'seq'), None, 'head'), parts along dimension 0, may hold values from -8 to 8
- cache_memory: bfloat16 [32768, 2, 1024], P(('groups', 'seq'), None, 'head'), parts along dimension 0, may hold values from -8 to 8
- block_mask: int32 [4, 128], P('groups', 'seq'), parts along dimension 0, may hold values 0 or 1
- owner_index: int32 [2], P('groups'), parts along dimension 0, may hold values from 0 to 3
- valid_count: int32 [2], P('groups'), parts along dimension 0, may hold values from 1 to 256
- output_weight: bfloat16 [4096, 4096], P('head', 'seq'), may hold values from -0.09375 to 0.09375
Outputs:
- mixed_output: float32 [512, 4096], P(('groups', 'head'), 'seq'), parts along dimension 0
The draws below stay inside these ranges and needn't reach their ends.
There are 2 independent parts, one for each index of `groups`. The reference program is written for one: setup_inputs(seed, part) draws one part's arguments, and reference() takes and returns one part's arrays. A program takes and returns all parts, laid end to end along the dimension named above; an argument that names none is the same for every part. Nothing has to cross between parts.
All inputs are finite; a program needn't handle non-finite values. No bound on the sum of `block_mask` on one device may be relied on, other than what follows from the above.
Results may differ from the reference program's by a relative error of at most 0.0065.
Values may be sent and summed in bfloat16 or wider, within the bound.
No kernel may reach another device: no remote copies, remote signals or barrier semaphores. Data moves between devices by JAX's collectives and lax.ppermute only.
A program may use at most 128 MiB of HBM per device.

```python
import jax
import jax.numpy as jnp
from jax import lax

D = 4096
HEADS = 32
KV_HEADS = 8
HD = 128
BLOCK = 128
SEGMENT = 256
CONTEXT = 16384
SLOTS = 1024
QBLOCKS = 2
KBLOCKS = 128
N_SEQ = 4


def draw_segment_query(key, part):
    fresh_key = jax.random.fold_in(key, 11)
    values = jnp.clip(1.75 * jax.random.normal(fresh_key, (SEGMENT, HEADS * HD), jnp.float32), -8.0, 8.0)
    return values.astype(jnp.bfloat16)


def draw_segment_memory(key, part):
    fresh_key = jax.random.fold_in(key, 13)
    values = jnp.clip(1.75 * jax.random.normal(fresh_key, (SEGMENT, 2, KV_HEADS * HD), jnp.float32), -8.0, 8.0)
    return values.astype(jnp.bfloat16)


def set_ends(drawn, rng, smallest, largest):
    extent = drawn.shape
    spot = [jax.random.randint(jax.random.fold_in(rng, axis), (), 0, extent[axis]) for axis in range(len(extent))]
    drawn = drawn.at[tuple(spot)].set(smallest)
    longest = extent.index(max(extent))
    spot[longest] = (spot[longest] + 1) % extent[longest]
    return drawn.at[tuple(spot)].set(largest)


def block_levels(stream_key, extent, cuts, smallest, largest):
    level = 1.0
    for dim, parts in cuts:
        draws = jax.random.uniform(jax.random.fold_in(jax.random.fold_in(stream_key, 6), dim), (parts,), jnp.float32, smallest / len(cuts), largest / len(cuts))
        level = level * jnp.repeat(jnp.exp(draws), extent[dim] // parts).reshape((-1,) + (1,) * (len(extent) - 1 - dim))
    return level


def scatter_about(key, shape, width, reach, pieces=(), dtype=jnp.bfloat16):
    values = jax.random.normal(key, shape, jnp.float32) * width
    if len(pieces) > 0:
        values = block_levels(key, shape, pieces, -0.22, 0.18) * values
    return jnp.clip(values, min=-reach, max=reach).astype(dtype)


def setup_inputs(seed: int = 0, part: int = 0) -> dict:
    arg_keys = jax.random.split(jax.random.key(seed), 9)
    own_keys = jax.random.split(jax.random.fold_in(arg_keys[8], part), 9)
    return {
        "segment_query": draw_segment_query(jax.random.fold_in(jax.random.fold_in(arg_keys[8], part), 71), part),
        "segment_memory": draw_segment_memory(jax.random.fold_in(jax.random.fold_in(arg_keys[8], part), 71), part),
        "finished_memory": scatter_about(own_keys[2], (SLOTS, 2, KV_HEADS * HD), 1.75, 8.0, ((0, 4), (2, 4))),
        "cache_memory": scatter_about(own_keys[3], (CONTEXT, 2, KV_HEADS * HD), 1.75, 8.0, ((0, 4), (2, 4))),
        "block_mask": set_ends((jax.random.randint(own_keys[4], (QBLOCKS, KBLOCKS), 0, 3) < 1).astype(jnp.int32), jax.random.fold_in(own_keys[4], 1), 0, 1),
        "owner_index": jax.random.randint(own_keys[5], (1,), 0, N_SEQ).astype(jnp.int32),
        "valid_count": jax.random.randint(own_keys[6], (1,), 1, SEGMENT + 1).astype(jnp.int32),
        "output_weight": scatter_about(arg_keys[7], (HEADS * HD, D), (HEADS * HD) ** -0.5, 0.09375, ((0, 4), (1, 4))),
    }


def reference(segment_query, segment_memory, finished_memory, cache_memory, block_mask, owner_index, valid_count, output_weight):
    group_size = HEADS // KV_HEADS
    slot_start = (owner_index[0] * SEGMENT).astype(jnp.int32)
    finished = lax.dynamic_slice_in_dim(finished_memory, slot_start, SEGMENT, 0)
    pairs = jnp.concatenate([cache_memory, finished, segment_memory], axis=0)
    key_rows = pairs[:, 0].reshape(-1, KV_HEADS, HD)
    value_rows = pairs[:, 1].reshape(-1, KV_HEADS, HD)
    context_ok = jnp.repeat(jnp.repeat(block_mask > 0, BLOCK, axis=0), BLOCK, axis=1)
    positions = jnp.arange(2 * SEGMENT)
    recent_ok = positions < SEGMENT + valid_count[0]
    allowed = jnp.concatenate([context_ok, jnp.broadcast_to(recent_ok[None, :], (SEGMENT, 2 * SEGMENT))], axis=1)
    queries = segment_query.reshape(SEGMENT, HEADS, HD)

    def one_head(head_number):
        query_rows = lax.dynamic_index_in_dim(queries, head_number, 1, keepdims=False)
        kv_number = head_number // group_size
        keys_here = lax.dynamic_index_in_dim(key_rows, kv_number, 1, keepdims=False)
        values_here = lax.dynamic_index_in_dim(value_rows, kv_number, 1, keepdims=False)
        scores = jnp.dot(query_rows, keys_here.T, preferred_element_type=jnp.float32) * (HD ** -0.5)
        scores = jnp.where(allowed, scores, -1.0e30)
        row_peak = jnp.max(scores, axis=1)
        weights = jnp.where(allowed, jnp.exp(scores - row_peak[:, None]), 0.0)
        row_total = jnp.sum(weights, axis=1)
        summed = jnp.dot(weights.astype(jnp.bfloat16), values_here, preferred_element_type=jnp.float32)
        return (summed / row_total[:, None]).astype(jnp.bfloat16)

    per_head = lax.map(one_head, jnp.arange(HEADS))
    attended = per_head.transpose(1, 0, 2).reshape(SEGMENT, HEADS * HD)
    return jnp.dot(attended, output_weight, preferred_element_type=jnp.float32)
```

```python
import functools
import math

import jax
import jax.numpy as jnp
from jax import lax
from jax.experimental import pallas as pl
from jax.experimental.pallas import tpu as pltpu
from jax.sharding import PartitionSpec as P

HD = 128
BLOCK = 128
LANES = 128
FLOOR = -1e30
LOW_PEAK = -1e29
SCALE = math.log2(math.e) / math.sqrt(HD)
BF = jnp.bfloat16
F32 = jnp.float32


def split_rows(raw, rows, kv, stage, keys_ref, values_ref, start):
    for g in range(kv):
        cols = pl.ds(g * HD, HD)
        stage[g, pl.ds(0, 2 * rows)] = raw[:, :, g * HD : (g + 1) * HD].reshape(2 * rows, HD).astype(F32)
        keys_ref[pl.ds(start, rows), cols] = stage[g, pl.ds(0, rows, stride=2)].astype(BF)
        values_ref[pl.ds(start, rows), cols] = stage[g, pl.ds(1, rows, stride=2)].astype(BF)


def prepare_body(kv, ctx_blocks, fin_blocks, own_rows, mask_ref, cache_ref, fin_ref, own_ref, keys_ref, values_ref, raw, stage, sems):
    def fetch(i):
        return pltpu.make_async_copy(cache_ref.at[pl.ds(i * BLOCK, BLOCK)], raw.at[i], sems.at[i])

    for i in range(ctx_blocks):
        fetch(i).start()
    own_start = (ctx_blocks + fin_blocks) * BLOCK
    pad = BLOCK - own_rows
    for ref in (keys_ref, values_ref):
        ref[pl.ds(own_start, BLOCK)] = jnp.zeros((BLOCK, kv * HD), BF)
    split_rows(own_ref[...], own_rows, kv, stage.at[0], keys_ref, values_ref, own_start)
    for i in range(fin_blocks):
        split_rows(fin_ref[pl.ds(i * BLOCK, BLOCK)], BLOCK, kv, stage.at[(i + 1) % 2], keys_ref, values_ref, (ctx_blocks + i) * BLOCK)

    @pl.loop(0, ctx_blocks)
    def _(i):
        fetch(i).wait()
        used = mask_ref[0, i]
        for q in range(1, mask_ref.shape[0]):
            used = used | mask_ref[q, i]

        @pl.when(used > 0)
        def _():
            split_rows(raw[i], BLOCK, kv, stage.at[i % 2], keys_ref, values_ref, pl.multiple_of(i * BLOCK, BLOCK))


def prepare(mask, cache, finished, own):
    rows, _, width = cache.shape
    kv = width // HD
    ctx_blocks, fin_blocks = rows // BLOCK, finished.shape[0] // BLOCK
    total = (ctx_blocks + fin_blocks + 1) * BLOCK
    vmem = pl.BlockSpec(memory_space=pltpu.VMEM)
    return pl.pallas_call(
        functools.partial(prepare_body, kv, ctx_blocks, fin_blocks, own.shape[0]),
        in_specs=[pl.BlockSpec(memory_space=pltpu.SMEM), pl.BlockSpec(memory_space=pl.ANY), vmem, vmem],
        out_specs=[vmem, vmem],
        out_shape=[jax.ShapeDtypeStruct((total, width), BF)] * 2,
        scratch_shapes=[
            pltpu.VMEM((ctx_blocks, BLOCK, 2, width), BF),
            pltpu.VMEM((2, kv, 2 * BLOCK, HD), F32),
            pltpu.SemaphoreType.DMA((ctx_blocks,)),
        ],
        cost_estimate=pl.CostEstimate(flops=0, bytes_accessed=12 * 1024 * 1024, transcendentals=0),
        compiler_params=pltpu.CompilerParams(vmem_limit_bytes=24 << 20),
        name="prepare",
    )(mask, cache, finished, own)


def attend_body(geometry, shifts, *refs):
    kv, group, tokens, ctx_blocks, fin_blocks, seq_blocks = geometry
    n = len(shifts)
    meta_ref, mask_ref, keys_ref, values_ref = refs[:4]
    query_refs, message_refs = refs[4 : 4 + n], refs[4 + n : 4 + 2 * n]
    blocks_ref, scores, peaks, totals, sums = refs[4 + 2 * n :]
    rows = group * tokens
    own_block = ctx_blocks + fin_blocks
    is_owner, limit = meta_ref[0], meta_ref[1]
    lane = lax.broadcasted_iota(jnp.int32, (1, 2 * BLOCK), 1)
    stat_lane = lax.broadcasted_iota(jnp.int32, (1, LANES), 1)

    for at, (query_ref, message_ref) in enumerate(zip(query_refs, message_refs, strict=True)):
        query_block = meta_ref[2 + at]

        def gather_block(i, count, query_block=query_block):
            blocks_ref[count] = i
            return count + jnp.where(mask_ref[query_block, i] > 0, 1, 0)

        count = lax.fori_loop(0, ctx_blocks, gather_block, jnp.int32(0))
        for i in range(fin_blocks):
            blocks_ref[count] = ctx_blocks + i
            count = count + is_owner
        blocks_ref[count] = own_block
        blocks_ref[count + 1] = own_block
        full = count
        pairs = (count + 2) // 2

        queries = [
            jnp.concatenate(
                [query_ref[:, (g * group + a) * HD : (g * group + a + 1) * HD] for a in range(group)], axis=0
            )
            for g in range(kv)
        ]

        def block_rows(ref, j, g):
            parts = [
                ref[pl.ds(pl.multiple_of(blocks_ref[2 * j + half] * BLOCK, BLOCK), BLOCK), g * HD : (g + 1) * HD]
                for half in range(2)
            ]
            return jnp.concatenate(parts, axis=0)

        def score(j, masked):
            for g in range(kv):
                s = lax.dot_general(
                    queries[g], block_rows(keys_ref, j, g), (((1,), (1,)), ((), ())), preferred_element_type=F32
                )
                if masked:
                    bound = jnp.where(2 * j < full, BLOCK, limit)
                    bound_next = jnp.where(2 * j + 1 < full, BLOCK, jnp.where(2 * j + 1 == full, limit, 0))
                    edge = jnp.where(lane < BLOCK, bound, BLOCK + bound_next)
                    s = s + jnp.where(lane < edge, 0.0, FLOOR)
                scores[j, g] = s
                peaks[g] = jnp.maximum(peaks[g], jnp.maximum(s[:, :BLOCK], s[:, BLOCK:]))

        peaks[...] = jnp.full(peaks.shape, LOW_PEAK, F32)
        pl.loop(0, pairs - 1)(lambda j: score(j, False))
        score(pairs - 1, True)

        shift = []
        for g in range(kv):
            peak = jnp.max(peaks[g], axis=1, keepdims=True) * SCALE
            shift.append(jnp.broadcast_to(peak.astype(BF).astype(F32), (rows, LANES)))
            peaks[g] = shift[g]
        totals[...] = jnp.zeros(totals.shape, F32)
        sums[...] = jnp.zeros(sums.shape, F32)

        @pl.loop(0, pairs)
        def _(j):
            for g in range(kv):
                s = scores[j, g]
                low = jnp.exp2(s[:, :BLOCK] * SCALE - peaks[g])
                high = jnp.exp2(s[:, BLOCK:] * SCALE - peaks[g])
                totals[g] += low + high
                weights = jnp.concatenate([low.astype(BF), high.astype(BF)], axis=1)
                sums[g] += jnp.dot(weights, block_rows(values_ref, j, g), preferred_element_type=F32)

        stats = jnp.zeros((tokens, LANES), F32)
        for g in range(kv):
            total = jnp.broadcast_to(jnp.sum(totals[g], axis=1, keepdims=True), (rows, LANES))
            coarse = total.astype(BF).astype(F32)
            for a in range(group):
                h = g * group + a
                part = slice(a * tokens, (a + 1) * tokens)
                message_ref[:, h * HD : (h + 1) * HD] = sums[g, part].astype(BF)
                stats = jnp.where(stat_lane == 3 * h, peaks[g, part], stats)
                stats = jnp.where(stat_lane == 3 * h + 1, coarse[part], stats)
                stats = jnp.where(stat_lane == 3 * h + 2, total[part] - coarse[part], stats)
        message_ref[:, kv * group * HD :] = stats.astype(BF)


def attend(meta, mask, keys, values, queries, kv, fin_blocks):
    tokens, width = queries[0].shape
    n = len(queries)
    group = width // (kv * HD)
    ctx_blocks = mask.shape[1]
    slots = ctx_blocks + fin_blocks + 2
    rows = group * tokens
    vmem, smem = pl.BlockSpec(memory_space=pltpu.VMEM), pl.BlockSpec(memory_space=pltpu.SMEM)
    geometry = (kv, group, tokens, ctx_blocks, fin_blocks, mask.shape[0])
    pair_count = (slots + 1) // 2
    return pl.pallas_call(
        functools.partial(attend_body, geometry, tuple(range(n))),
        in_specs=[smem, smem] + [vmem] * (2 + n),
        out_specs=[vmem] * n,
        out_shape=[jax.ShapeDtypeStruct((tokens, width + LANES), BF)] * n,
        scratch_shapes=[
            pltpu.SMEM((slots + 1,), jnp.int32),
            pltpu.VMEM((pair_count, kv, rows, 2 * BLOCK), F32),
            pltpu.VMEM((kv, rows, LANES), F32),
            pltpu.VMEM((kv, rows, LANES), F32),
            pltpu.VMEM((kv, rows, HD), F32),
        ],
        cost_estimate=pl.CostEstimate(
            flops=4 * n * rows * kv * HD * BLOCK * slots // 2,
            bytes_accessed=2 * keys.size * 2,
            transcendentals=n * rows * kv * BLOCK * slots // 2,
        ),
        compiler_params=pltpu.CompilerParams(vmem_limit_bytes=28 << 20),
        name="attend",
    )(meta, mask, keys, values, *queries)


def merge_body(heads, *refs):
    *parts, out_ref = refs
    loaded = [part[:, heads * HD :].astype(F32) for part in parts]
    for h in range(heads):
        peaks = [s[:, 3 * h : 3 * h + 1] for s in loaded]
        totals = [s[:, 3 * h + 1 : 3 * h + 2] + s[:, 3 * h + 2 : 3 * h + 3] for s in loaded]
        top = functools.reduce(jnp.maximum, peaks)
        factors = [jnp.exp2(p - top) for p in peaks]
        inverse = 1.0 / sum(f * t for f, t in zip(factors, totals, strict=True))
        cols = slice(h * HD, (h + 1) * HD)
        out_ref[:, cols] = sum(
            part[:, cols].astype(F32) * (f * inverse) for part, f in zip(parts, factors, strict=True)
        ).astype(BF)


def merge(parts, heads):
    tokens = parts[0].shape[0]
    return pl.pallas_call(
        functools.partial(merge_body, heads),
        in_specs=[pl.BlockSpec(memory_space=pltpu.VMEM)] * len(parts),
        out_specs=pl.BlockSpec(memory_space=pltpu.VMEM),
        out_shape=jax.ShapeDtypeStruct((tokens, heads * HD), BF),
        compiler_params=pltpu.CompilerParams(vmem_limit_bytes=16 << 20),
        name="merge",
    )(*parts)


def per_device(
    n_seq,
    n_head,
    segment_query,
    segment_memory,
    finished_memory,
    cache_memory,
    block_mask,
    owner_index,
    valid_count,
    output_weight,
):
    here = lax.axis_index("seq")
    own_tokens, width = segment_query.shape
    heads = width // HD
    kv = segment_memory.shape[2] // HD
    fin_blocks = finished_memory.shape[0] // BLOCK
    direct = n_seq == 4 and n_head == 4

    is_owner = (here == owner_index[0]).astype(jnp.int32)
    limit = jnp.clip(valid_count[0] - here * own_tokens, 0, own_tokens)

    if direct:
        def toward(k):
            return [(i, i ^ k) for i in range(n_seq)]

        queries = [segment_query] + [lax.ppermute(segment_query, "seq", toward(k)) for k in range(1, n_seq)]
        query_blocks = [((here ^ k) * own_tokens) // BLOCK for k in range(n_seq)]
    else:
        gathered = lax.all_gather(segment_query, "seq", axis=0, tiled=True)
        query_blocks = list(range(gathered.shape[0] // BLOCK))
        queries = [gathered[i * BLOCK : (i + 1) * BLOCK] for i in query_blocks]

    meta = jnp.stack([jnp.asarray(x, jnp.int32) for x in [is_owner, limit] + query_blocks])
    keys, values = prepare(block_mask, cache_memory, finished_memory, segment_memory)
    messages = attend(meta, block_mask, keys, values, queries, kv, fin_blocks)

    if direct:
        parts = [messages[0]] + [lax.ppermute(messages[k], "seq", toward(k)) for k in range(1, n_seq)]
        attended = merge(parts, heads)
        shards = [attended] + [lax.ppermute(attended, "seq", toward(k)) for k in range(1, n_seq)]
        stacked = jnp.stack(shards)
        projected = jnp.einsum("ktf,fd->ktd", stacked, output_weight, preferred_element_type=F32)
        head_at = lax.axis_index("head")
        tile = projected.shape[1:]
        core, side = head_at % 2, head_at // 2

        def shard_of(token_shard):
            return lax.dynamic_index_in_dim(projected, token_shard ^ here, 0, keepdims=False)

        mine_core = [shard_of(core), shard_of(2 + core)]
        other_core = jnp.stack([shard_of(1 - core), shard_of(3 - core)]).astype(BF)
        received = lax.ppermute(other_core, "head", [(i, i ^ 1) for i in range(n_head)])
        joined = jnp.stack(mine_core) + received.astype(F32)
        mine = lax.dynamic_index_in_dim(joined, side, 0, keepdims=False)
        other = lax.dynamic_index_in_dim(joined, 1 - side, 0, keepdims=False).astype(BF)
        return mine + lax.ppermute(other, "head", [(i, i ^ 2) for i in range(n_head)]).astype(F32)

    sent = jnp.concatenate(messages, axis=0)
    got = lax.all_to_all(sent, "seq", 0, 0, tiled=True).reshape(n_seq, own_tokens, -1)
    attended = merge([got[i] for i in range(n_seq)], heads)
    attended = lax.all_gather(attended, "seq", axis=0, tiled=True)
    return lax.psum_scatter(
        jnp.dot(attended, output_weight, preferred_element_type=F32), "head", scatter_dimension=0, tiled=True
    )


def solution(mesh):
    return jax.shard_map(
        functools.partial(per_device, mesh.shape["seq"], mesh.shape["head"]),
        mesh=mesh,
        in_specs=(
            P(("groups", "seq"), "head"),
            P(("groups", "seq"), None, "head"),
            P(("groups", "seq"), None, "head"),
            P(("groups", "seq"), None, "head"),
            P("groups", "seq"),
            P("groups"),
            P("groups"),
            P("head", "seq"),
        ),
        out_specs=P(("groups", "head"), "seq"),
        check_vma=False,
    )
```

```python
import functools
import math

import jax
import jax.numpy as jnp
from jax import lax
from jax.experimental import pallas as pl
from jax.experimental.pallas import tpu as pltpu
from jax.sharding import PartitionSpec as P

HD = 128
BLOCK = 128
LANES = 128
FLOOR = -1e30
LOW_PEAK = -1e29
SCALE = math.log2(math.e) / math.sqrt(HD)
BF = jnp.bfloat16
F32 = jnp.float32


VMEM_LIMIT = 30 << 20
UNROLL = 4


def params():
    return pltpu.CompilerParams(vmem_limit_bytes=VMEM_LIMIT)


def vmem_spec():
    return pl.BlockSpec(memory_space=pltpu.VMEM)


def smem_spec():
    return pl.BlockSpec(memory_space=pltpu.SMEM)


def prepare_body(ctx_blocks, fin_blocks, own_rows, mask_ref, cache_ref, fin_ref, own_ref, keys_ref, values_ref, used_ref):
    width = keys_ref.shape[1]
    row = lax.broadcasted_iota(jnp.int32, (2 * BLOCK, 2 * BLOCK), 0)
    col = lax.broadcasted_iota(jnp.int32, (2 * BLOCK, 2 * BLOCK), 1)
    source = jnp.where(row < BLOCK, 2 * row, 2 * row - 2 * BLOCK + 1)
    pick = jnp.where(col == source, 1.0, 0.0).astype(BF)

    def take_apart(pairs, start):
        parts = jnp.dot(pick, pairs.reshape(2 * BLOCK, width), preferred_element_type=F32).astype(BF)
        keys_ref[pl.ds(start, BLOCK)] = parts[:BLOCK]
        values_ref[pl.ds(start, BLOCK)] = parts[BLOCK:]

    def note(i, count):
        used_ref[count] = i
        used = mask_ref[0, i]
        for q in range(1, mask_ref.shape[0]):
            used = used | mask_ref[q, i]
        return count + jnp.where(used > 0, 1, 0)

    count = lax.fori_loop(0, ctx_blocks, note, jnp.int32(0))
    for i in range(UNROLL):
        used_ref[count + i] = ctx_blocks - 1

    @pl.loop(0, (count + UNROLL - 1) // UNROLL)
    def _(j):
        for i in range(UNROLL):
            start = pl.multiple_of(used_ref[j * UNROLL + i] * BLOCK, BLOCK)
            take_apart(cache_ref[pl.ds(start, BLOCK)], start)

    for i in range(fin_blocks):
        take_apart(fin_ref[pl.ds(i * BLOCK, BLOCK)], (ctx_blocks + i) * BLOCK)
    own = jnp.concatenate([own_ref[...], jnp.zeros((BLOCK - own_rows, 2, width), BF)], axis=0)
    take_apart(own, (ctx_blocks + fin_blocks) * BLOCK)


def prepare(mask, cache, finished, own):
    rows, _, width = cache.shape
    ctx_blocks, fin_blocks = rows // BLOCK, finished.shape[0] // BLOCK
    total = (ctx_blocks + fin_blocks + 1) * BLOCK
    return pl.pallas_call(
        functools.partial(prepare_body, ctx_blocks, fin_blocks, own.shape[0]),
        in_specs=[smem_spec(), vmem_spec(), vmem_spec(), vmem_spec()],
        out_specs=[vmem_spec(), vmem_spec()],
        out_shape=[jax.ShapeDtypeStruct((total, width), BF)] * 2,
        scratch_shapes=[pltpu.SMEM((ctx_blocks + UNROLL,), jnp.int32)],
        cost_estimate=pl.CostEstimate(flops=0, bytes_accessed=12 * 1024 * 1024, transcendentals=0),
        compiler_params=params(),
        name="prepare",
    )(mask, cache, finished, own)


def attend_body(geometry, *refs):
    kv, group, tokens, ctx_blocks, fin_blocks, n = geometry
    meta_ref, mask_ref, keys_ref, values_ref = refs[:4]
    query_refs, message_refs = refs[4 : 4 + n], refs[4 + n : 4 + 2 * n]
    blocks_ref, scores, peaks, totals, sums = refs[4 + 2 * n :]
    rows = n * group * tokens
    own_block = ctx_blocks + fin_blocks
    is_owner, limit, query_block = meta_ref[0], meta_ref[1], meta_ref[2]
    lane = lax.broadcasted_iota(jnp.int32, (1, 2 * BLOCK), 1)
    stat_lane = lax.broadcasted_iota(jnp.int32, (1, LANES), 1)

    def gather_block(i, count):
        blocks_ref[count] = i
        return count + jnp.where(mask_ref[query_block, i] > 0, 1, 0)

    full = lax.fori_loop(0, ctx_blocks, gather_block, jnp.int32(0))
    for i in range(fin_blocks):
        blocks_ref[full] = ctx_blocks + i
        full = full + is_owner
    blocks_ref[full] = own_block
    blocks_ref[full + 1] = own_block
    pairs = (full + 2) // 2

    def cols(h):
        return slice(h * HD, (h + 1) * HD)

    queries = [
        jnp.concatenate([ref[:, cols(g * group + a)] for ref in query_refs for a in range(group)], axis=0)
        for g in range(kv)
    ]

    def block_rows(ref, j, g, count):
        parts = [
            ref[pl.ds(pl.multiple_of(blocks_ref[2 * j + i] * BLOCK, BLOCK), BLOCK), cols(g)] for i in range(2 * count)
        ]
        return jnp.concatenate(parts, axis=0)

    def score(j, count, masked):
        for g in range(kv):
            top = peaks[g]
            for i in range(count):
                s = lax.dot_general(
                    queries[g], block_rows(keys_ref, j + i, g, 1), (((1,), (1,)), ((), ())), preferred_element_type=F32
                )
                if masked:
                    bound = jnp.where(2 * j < full, BLOCK, limit)
                    bound_next = jnp.where(2 * j + 1 == full, limit, 0)
                    edge = jnp.where(lane < BLOCK, bound, BLOCK + bound_next)
                    s = s + jnp.where(lane < edge, 0.0, FLOOR)
                scores[j + i, g] = s
                top = jnp.maximum(top, jnp.maximum(s[:, :BLOCK], s[:, BLOCK:]))
            peaks[g] = top

    def accumulate(j, count):
        for g in range(kv):
            total, weights = totals[g], []
            for i in range(count):
                s = scores[j + i, g]
                for half in range(2):
                    w = jnp.exp2(s[:, half * BLOCK : (half + 1) * BLOCK] * SCALE - peaks[g])
                    total = total + w
                    weights.append(w.astype(BF))
            totals[g] = total
            sums[g] += jnp.dot(
                jnp.concatenate(weights, axis=1), block_rows(values_ref, j, g, count), preferred_element_type=F32
            )

    def by_twos(total, step):
        pl.loop(0, total // 2)(lambda j: step(2 * j, 2))
        pl.when(total % 2 == 1)(lambda: step(total - 1, 1))

    peaks[...] = jnp.full(peaks.shape, LOW_PEAK, F32)
    by_twos(pairs - 1, lambda j, count: score(j, count, False))
    score(pairs - 1, 1, True)

    for g in range(kv):
        peak = jnp.max(peaks[g], axis=1, keepdims=True) * SCALE
        peaks[g] = jnp.broadcast_to(peak.astype(BF).astype(F32), (rows, LANES))
    totals[...] = jnp.zeros(totals.shape, F32)
    sums[...] = jnp.zeros(sums.shape, F32)
    by_twos(pairs, accumulate)

    stats = [jnp.zeros((tokens, LANES), F32) for _ in range(n)]
    for g in range(kv):
        total = jnp.broadcast_to(jnp.sum(totals[g], axis=1, keepdims=True), (rows, LANES))
        coarse = total.astype(BF).astype(F32)
        for r in range(n):
            for a in range(group):
                h = g * group + a
                part = slice((r * group + a) * tokens, (r * group + a + 1) * tokens)
                message_refs[r][:, cols(h)] = sums[g, part].astype(BF)
                for at, value in enumerate((peaks[g, part], coarse[part], total[part] - coarse[part])):
                    stats[r] = jnp.where(stat_lane == 3 * h + at, value, stats[r])
    for r in range(n):
        message_refs[r][:, kv * group * HD :] = stats[r].astype(BF)


def attend(meta, mask, keys, values, queries, kv, fin_blocks):
    tokens, width = queries[0].shape
    n = len(queries)
    group = width // (kv * HD)
    ctx_blocks = mask.shape[1]
    slots = ctx_blocks + fin_blocks + 2
    rows = n * group * tokens
    return pl.pallas_call(
        functools.partial(attend_body, (kv, group, tokens, ctx_blocks, fin_blocks, n)),
        in_specs=[smem_spec(), smem_spec()] + [vmem_spec()] * (2 + n),
        out_specs=[vmem_spec()] * n,
        out_shape=[jax.ShapeDtypeStruct((tokens, width + LANES), BF)] * n,
        scratch_shapes=[
            pltpu.SMEM((slots + 1,), jnp.int32),
            pltpu.VMEM(((slots + 1) // 2, kv, rows, 2 * BLOCK), F32),
            pltpu.VMEM((kv, rows, LANES), F32),
            pltpu.VMEM((kv, rows, LANES), F32),
            pltpu.VMEM((kv, rows, HD), F32),
        ],
        cost_estimate=pl.CostEstimate(
            flops=4 * rows * kv * HD * BLOCK * slots // 2,
            bytes_accessed=2 * keys.size * 2,
            transcendentals=rows * kv * BLOCK * slots // 2,
        ),
        compiler_params=params(),
        name="attend",
    )(meta, mask, keys, values, *queries)


def merge_body(heads, *refs):
    *parts, out_ref = refs
    loaded = [part[:, heads * HD :].astype(F32) for part in parts]
    for h in range(heads):
        peaks = [s[:, 3 * h : 3 * h + 1] for s in loaded]
        totals = [s[:, 3 * h + 1 : 3 * h + 2] + s[:, 3 * h + 2 : 3 * h + 3] for s in loaded]
        top = functools.reduce(jnp.maximum, peaks)
        factors = [jnp.exp2(p - top) for p in peaks]
        inverse = 1.0 / sum(f * t for f, t in zip(factors, totals, strict=True))
        cols = slice(h * HD, (h + 1) * HD)
        out_ref[:, cols] = sum(
            part[:, cols].astype(F32) * (f * inverse) for part, f in zip(parts, factors, strict=True)
        ).astype(BF)


def merge(parts, heads):
    tokens = parts[0].shape[0]
    return pl.pallas_call(
        functools.partial(merge_body, heads),
        in_specs=[pl.BlockSpec(memory_space=pltpu.VMEM)] * len(parts),
        out_specs=pl.BlockSpec(memory_space=pltpu.VMEM),
        out_shape=jax.ShapeDtypeStruct((tokens, heads * HD), BF),
        compiler_params=params(),
        name="merge",
    )(*parts)


def per_device(
    n_seq,
    n_head,
    segment_query,
    segment_memory,
    finished_memory,
    cache_memory,
    block_mask,
    owner_index,
    valid_count,
    output_weight,
):
    here = lax.axis_index("seq")
    own_tokens, width = segment_query.shape
    heads = width // HD
    kv = segment_memory.shape[2] // HD
    fin_blocks = finished_memory.shape[0] // BLOCK
    direct = n_seq == 4 and n_head == 4 and BLOCK == 2 * own_tokens

    is_owner = (here == owner_index[0]).astype(jnp.int32)
    limit = jnp.clip(valid_count[0] - here * own_tokens, 0, own_tokens)

    if direct:
        def toward(k):
            return [(i, i ^ k) for i in range(n_seq)]

        queries = [segment_query] + [lax.ppermute(segment_query, "seq", toward(k)) for k in range(1, n_seq)]
        per_block = BLOCK // own_tokens
        batches = [(((here ^ k) * own_tokens) // BLOCK, queries[k : k + per_block]) for k in range(0, n_seq, per_block)]
    else:
        gathered = lax.all_gather(segment_query, "seq", axis=0, tiled=True)
        batches = [(i, [gathered[i * BLOCK : (i + 1) * BLOCK]]) for i in range(gathered.shape[0] // BLOCK)]

    keys, values = prepare(block_mask, cache_memory, finished_memory, segment_memory)
    messages = []
    for query_block, queries in batches:
        meta = jnp.stack([is_owner, limit, jnp.asarray(query_block, jnp.int32)])
        messages += attend(meta, block_mask, keys, values, queries, kv, fin_blocks)

    if direct:
        parts = [messages[0]] + [lax.ppermute(messages[k], "seq", toward(k)) for k in range(1, n_seq)]
        attended = merge(parts, heads)
        shards = [attended] + [lax.ppermute(attended, "seq", toward(k)) for k in range(1, n_seq)]
        stacked = jnp.stack(shards)
        projected = jnp.einsum("ktf,fd->ktd", stacked, output_weight, preferred_element_type=F32)
        head_at = lax.axis_index("head")
        tile = projected.shape[1:]
        core, side = head_at % 2, head_at // 2

        def shard_of(token_shard):
            return lax.dynamic_index_in_dim(projected, token_shard ^ here, 0, keepdims=False)

        mine_core = [shard_of(core), shard_of(2 + core)]
        other_core = jnp.stack([shard_of(1 - core), shard_of(3 - core)]).astype(BF)
        received = lax.ppermute(other_core, "head", [(i, i ^ 1) for i in range(n_head)])
        joined = jnp.stack(mine_core) + received.astype(F32)
        mine = lax.dynamic_index_in_dim(joined, side, 0, keepdims=False)
        other = lax.dynamic_index_in_dim(joined, 1 - side, 0, keepdims=False).astype(BF)
        return mine + lax.ppermute(other, "head", [(i, i ^ 2) for i in range(n_head)]).astype(F32)

    sent = jnp.concatenate(messages, axis=0)
    got = lax.all_to_all(sent, "seq", 0, 0, tiled=True).reshape(n_seq, own_tokens, -1)
    attended = merge([got[i] for i in range(n_seq)], heads)
    attended = lax.all_gather(attended, "seq", axis=0, tiled=True)
    return lax.psum_scatter(
        jnp.dot(attended, output_weight, preferred_element_type=F32), "head", scatter_dimension=0, tiled=True
    )


def solution(mesh):
    return jax.shard_map(
        functools.partial(per_device, mesh.shape["seq"], mesh.shape["head"]),
        mesh=mesh,
        in_specs=(
            P(("groups", "seq"), "head"),
            P(("groups", "seq"), None, "head"),
            P(("groups", "seq"), None, "head"),
            P(("groups", "seq"), None, "head"),
            P("groups", "seq"),
            P("groups"),
            P("groups"),
            P("head", "seq"),
        ),
        out_specs=P(("groups", "head"), "seq"),
        check_vma=False,
    )
```

```python
import functools
import math

import jax
import jax.numpy as jnp
from jax import lax
from jax.experimental import pallas as pl
from jax.experimental.pallas import tpu as pltpu
from jax.sharding import PartitionSpec as P

HD = 128
BLOCK = 128
LANES = 128
FLOOR = -1e30
LOW_PEAK = -1e29
SCALE = math.log2(math.e) / math.sqrt(HD)
BF = jnp.bfloat16
F32 = jnp.float32


VMEM_LIMIT = 26 << 20
UNROLL = 4


def params():
    return pltpu.CompilerParams(vmem_limit_bytes=VMEM_LIMIT)


def vmem_spec():
    return pl.BlockSpec(memory_space=pltpu.VMEM)


def smem_spec():
    return pl.BlockSpec(memory_space=pltpu.SMEM)


def list_body(fin_blocks, heading, meta_ref, lists_ref):
    query_blocks, ctx_blocks = meta_ref.shape[0] - 1, meta_ref.shape[1]
    end = lists_ref.shape[1] - 1
    own_block = ctx_blocks + fin_blocks

    def note(i, counts):
        bits = [meta_ref[q, i] for q in range(query_blocks)]
        bits.append(functools.reduce(lambda x, y: x | y, bits))
        for q, count in enumerate(counts):
            lists_ref[q, count] = i
        return tuple(count + jnp.where(bit > 0, 1, 0) for count, bit in zip(counts, bits, strict=True))

    counts = lax.fori_loop(0, ctx_blocks, note, (jnp.int32(0),) * (query_blocks + 1))
    for q, count in enumerate(counts[:-1]):
        for i in range(fin_blocks):
            lists_ref[q, count] = ctx_blocks + i
            count = count + meta_ref[query_blocks, 0]
        lists_ref[q, count] = own_block
        lists_ref[q, count + 1] = own_block
        lists_ref[q, end] = count
    for i in range(UNROLL - 1):
        lists_ref[query_blocks, counts[-1] + i] = ctx_blocks - 1
    lists_ref[query_blocks, end] = counts[-1]
    for i in range(heading):
        lists_ref[query_blocks + 1, i] = meta_ref[query_blocks, i]


def make_lists(meta, fin_blocks, heading):
    query_blocks, ctx_blocks = meta.shape[0] - 1, meta.shape[1]
    shape = (query_blocks + 2, ctx_blocks + fin_blocks + UNROLL + 2)
    return pl.pallas_call(
        functools.partial(list_body, fin_blocks, heading),
        in_specs=[smem_spec()],
        out_specs=smem_spec(),
        out_shape=jax.ShapeDtypeStruct(shape, jnp.int32),
        cost_estimate=pl.CostEstimate(flops=4 * 1024**3, bytes_accessed=0, transcendentals=0),
        compiler_params=params(),
        name="lists",
    )(meta)


def prepare_body(ctx_blocks, lists_ref, cache_ref, fin_ref, own_ref, keys_ref, values_ref):
    width = keys_ref.shape[1]
    any_row, end = lists_ref.shape[0] - 2, lists_ref.shape[1] - 1
    row = lax.broadcasted_iota(jnp.int32, (2 * BLOCK, 2 * BLOCK), 0)
    col = lax.broadcasted_iota(jnp.int32, (2 * BLOCK, 2 * BLOCK), 1)
    source = jnp.where(row < BLOCK, 2 * row, 2 * row - 2 * BLOCK + 1)
    pick = jnp.where(col == source, 1.0, 0.0).astype(BF)

    def take_apart(pairs, start):
        parts = jnp.dot(pick, pairs.reshape(2 * BLOCK, width), preferred_element_type=F32).astype(BF)
        keys_ref[pl.ds(start, BLOCK)] = parts[:BLOCK]
        values_ref[pl.ds(start, BLOCK)] = parts[BLOCK:]

    @pl.loop(0, (lists_ref[any_row, end] + UNROLL - 1) // UNROLL)
    def _(j):
        for i in range(UNROLL):
            start = pl.multiple_of(lists_ref[any_row, j * UNROLL + i] * BLOCK, BLOCK)
            take_apart(cache_ref[pl.ds(start, BLOCK)], start)

    fin_blocks, own_rows = fin_ref.shape[0] // BLOCK, own_ref.shape[0]
    for i in range(fin_blocks):
        take_apart(fin_ref[i * BLOCK : (i + 1) * BLOCK], (ctx_blocks + i) * BLOCK)
    filler = jnp.zeros((BLOCK - own_rows, 2, width), BF)
    take_apart(jnp.concatenate([own_ref[...], filler], axis=0), (ctx_blocks + fin_blocks) * BLOCK)


def prepare(lists, cache, finished, own):
    rows, _, width = cache.shape
    total = rows + finished.shape[0] + BLOCK
    return pl.pallas_call(
        functools.partial(prepare_body, rows // BLOCK),
        in_specs=[smem_spec(), vmem_spec(), vmem_spec(), vmem_spec()],
        out_specs=[vmem_spec(), vmem_spec()],
        out_shape=[jax.ShapeDtypeStruct((total, width), BF)] * 2,
        cost_estimate=pl.CostEstimate(flops=4 * 1024**3, bytes_accessed=12 * 1024**2, transcendentals=0),
        compiler_params=params(),
        name="prepare",
    )(lists, cache, finished, own)


def attend_body(geometry, *refs):
    kv, group, tokens, n, at = geometry
    lists_ref, keys_ref, values_ref = refs[:3]
    query_refs, message_refs = refs[3 : 3 + n], refs[4 + n : 4 + 2 * n]
    scores, peaks, totals, sums = refs[4 + 2 * n :]
    rows = n * group * tokens
    heading = lists_ref.shape[0] - 1
    limit, query_block = lists_ref[heading, 1], lists_ref[heading, 2 + at]
    full = lists_ref[query_block, lists_ref.shape[1] - 1]
    pairs = (full + 2) // 2
    lane = lax.broadcasted_iota(jnp.int32, (1, 2 * BLOCK), 1)
    stat_lane = lax.broadcasted_iota(jnp.int32, (1, LANES), 1)

    def cols(h):
        return slice(h * HD, (h + 1) * HD)

    queries = [
        jnp.concatenate([ref[:, cols(g * group + a)] for ref in query_refs for a in range(group)], axis=0)
        for g in range(kv)
    ]

    def block_rows(ref, j, g, count):
        parts = [
            ref[pl.ds(pl.multiple_of(lists_ref[query_block, 2 * j + i] * BLOCK, BLOCK), BLOCK), cols(g)] for i in range(2 * count)
        ]
        return jnp.concatenate(parts, axis=0)

    def score(j, count, masked):
        for g in range(kv):
            top = peaks[g]
            for i in range(count):
                s = lax.dot_general(
                    queries[g], block_rows(keys_ref, j + i, g, 1), (((1,), (1,)), ((), ())), preferred_element_type=F32
                )
                if masked:
                    bound = jnp.where(2 * j < full, BLOCK, limit)
                    bound_next = jnp.where(2 * j + 1 == full, limit, 0)
                    edge = jnp.where(lane < BLOCK, bound, BLOCK + bound_next)
                    s = s + jnp.where(lane < edge, 0.0, FLOOR)
                scores[j + i, g] = s
                top = jnp.maximum(top, jnp.maximum(s[:, :BLOCK], s[:, BLOCK:]))
            peaks[g] = top

    def accumulate(j, count):
        for g in range(kv):
            total, weights = totals[g], []
            for i in range(count):
                s = scores[j + i, g]
                for half in range(2):
                    w = jnp.exp2(s[:, half * BLOCK : (half + 1) * BLOCK] * SCALE - peaks[g])
                    total = total + w
                    weights.append(w.astype(BF))
            totals[g] = total
            sums[g] += jnp.dot(
                jnp.concatenate(weights, axis=1), block_rows(values_ref, j, g, count), preferred_element_type=F32
            )

    def in_steps(total, step):
        pl.loop(0, total // 4)(lambda j: step(4 * j, 4))
        done = total // 4 * 4
        pl.when(total - done >= 2)(lambda: step(done, 2))
        pl.when(total % 2 == 1)(lambda: step(total - 1, 1))

    peaks[...] = jnp.full(peaks.shape, LOW_PEAK, F32)
    in_steps(pairs - 1, lambda j, count: score(j, count, False))
    score(pairs - 1, 1, True)

    for g in range(kv):
        peak = jnp.max(peaks[g], axis=1, keepdims=True) * SCALE
        peaks[g] = jnp.broadcast_to(peak.astype(BF).astype(F32), (rows, LANES))
    totals[...] = jnp.zeros(totals.shape, F32)
    sums[...] = jnp.zeros(sums.shape, F32)
    in_steps(pairs, accumulate)

    stats = [jnp.zeros((tokens, LANES), F32) for _ in range(n)]
    for g in range(kv):
        total = jnp.broadcast_to(jnp.sum(totals[g], axis=1, keepdims=True), (rows, LANES))
        coarse = total.astype(BF).astype(F32)
        for r in range(n):
            for a in range(group):
                h = g * group + a
                part = slice((r * group + a) * tokens, (r * group + a + 1) * tokens)
                message_refs[r][:, cols(h)] = sums[g, part].astype(BF)
                for at, value in enumerate((peaks[g, part], coarse[part], total[part] - coarse[part])):
                    stats[r] = jnp.where(stat_lane == 3 * h + at, value, stats[r])
    for r in range(n):
        message_refs[r][:, kv * group * HD :] = stats[r].astype(BF)


def attend(lists, keys, values, queries, after, kv, at):
    tokens, width = queries[0].shape
    n = len(queries)
    group = width // (kv * HD)
    slots = keys.shape[0] // BLOCK + 1
    rows = n * group * tokens
    return pl.pallas_call(
        functools.partial(attend_body, (kv, group, tokens, n, at)),
        in_specs=[smem_spec()] + [vmem_spec()] * (2 + n) + [pl.BlockSpec(memory_space=pl.ANY)],
        out_specs=[vmem_spec()] * n,
        out_shape=[jax.ShapeDtypeStruct((tokens, width + LANES), BF)] * n,
        scratch_shapes=[
            pltpu.VMEM(((slots + 1) // 2, kv, rows, 2 * BLOCK), F32),
            pltpu.VMEM((kv, rows, LANES), F32),
            pltpu.VMEM((kv, rows, LANES), F32),
            pltpu.VMEM((kv, rows, HD), F32),
        ],
        cost_estimate=pl.CostEstimate(
            flops=4 * rows * kv * HD * BLOCK * slots // 2,
            bytes_accessed=2 * keys.size * 2,
            transcendentals=rows * kv * BLOCK * slots // 2,
        ),
        compiler_params=params(),
        name="attend",
    )(lists, keys, values, *queries, after)


def merge_body(heads, *refs):
    *parts, out_ref = refs
    loaded = [part[:, heads * HD :].astype(F32) for part in parts]
    for h in range(heads):
        peaks = [s[:, 3 * h : 3 * h + 1] for s in loaded]
        totals = [s[:, 3 * h + 1 : 3 * h + 2] + s[:, 3 * h + 2 : 3 * h + 3] for s in loaded]
        top = functools.reduce(jnp.maximum, peaks)
        factors = [jnp.exp2(p - top) for p in peaks]
        inverse = 1.0 / sum(f * t for f, t in zip(factors, totals, strict=True))
        cols = slice(h * HD, (h + 1) * HD)
        out_ref[:, cols] = sum(
            part[:, cols].astype(F32) * (f * inverse) for part, f in zip(parts, factors, strict=True)
        ).astype(BF)


def merge(parts, heads):
    tokens = parts[0].shape[0]
    return pl.pallas_call(
        functools.partial(merge_body, heads),
        in_specs=[pl.BlockSpec(memory_space=pltpu.VMEM)] * len(parts),
        out_specs=pl.BlockSpec(memory_space=pltpu.VMEM),
        out_shape=jax.ShapeDtypeStruct((tokens, heads * HD), BF),
        compiler_params=params(),
        name="merge",
    )(*parts)


def per_device(
    n_seq,
    n_head,
    segment_query,
    segment_memory,
    finished_memory,
    cache_memory,
    block_mask,
    owner_index,
    valid_count,
    output_weight,
):
    here = lax.axis_index("seq")
    own_tokens, width = segment_query.shape
    heads = width // HD
    kv = segment_memory.shape[2] // HD
    fin_blocks = finished_memory.shape[0] // BLOCK
    direct = n_seq == 4 and n_head == 4 and BLOCK == 2 * own_tokens

    is_owner = (here == owner_index[0]).astype(jnp.int32)
    limit = jnp.clip(valid_count[0] - here * own_tokens, 0, own_tokens)

    def swap(value, axis, size, k):
        return lax.ppermute(value, axis, [(i, i ^ k) for i in range(size)])

    def gather_over_seq(value):
        near, far = swap(value, "seq", n_seq, 1), swap(value, "seq", n_seq, 2)
        return [value, near, far, swap(far, "seq", n_seq, 1)]

    if direct:
        batches = ((2,), (3,), (1,), (0,))
        query_blocks = [((here ^ batch[0]) * own_tokens) // BLOCK for batch in batches]
    else:
        query_blocks = list(range(own_tokens * n_seq // BLOCK))
    heading = jnp.stack([jnp.asarray(x, jnp.int32) for x in [is_owner, limit] + query_blocks])
    heading_row = jnp.pad(heading, (0, block_mask.shape[1] - heading.shape[0]))
    lists = make_lists(jnp.concatenate([block_mask, heading_row[None]]), fin_blocks, heading.shape[0])

    if direct:
        order = [k for batch in batches for k in batch]
        arrived = gather_over_seq(segment_query)
        queries = [[arrived[k] for k in batch] for batch in batches]
    else:
        gathered = lax.all_gather(segment_query, "seq", axis=0, tiled=True)
        queries = [[gathered[i * BLOCK : (i + 1) * BLOCK]] for i in query_blocks]

    keys, values = prepare(lists, cache_memory, finished_memory, segment_memory)
    messages = []
    for at, batch in enumerate(queries):
        messages += attend(lists, keys, values, batch, messages[-1] if messages else lists, kv, at)

    if direct:
        parts = [m if k == 0 else swap(m, "seq", n_seq, k) for k, m in zip(order, messages, strict=True)]
        attended = merge(parts, heads)

        shards = gather_over_seq(attended)
        head_at = lax.axis_index("head")
        core, side = head_at % 2, head_at // 2

        def project(rows):
            return jnp.dot(rows, output_weight, preferred_element_type=F32)

        def over_cores(pair):
            first_mine = (here ^ pair[0]) % 2 == core
            first, second = shards[pair[0]], shards[pair[1]]
            other = project(jnp.where(first_mine, second, first)).astype(BF)
            mine = project(jnp.where(first_mine, first, second))
            return mine + swap(other, "head", n_head, 1).astype(F32)

        near, far = over_cores((0, 1)), over_cores((2, 3))
        near_mine = here // 2 == side
        mine, other = jnp.where(near_mine, near, far), jnp.where(near_mine, far, near)
        return mine + swap(other.astype(BF), "head", n_head, 2).astype(F32)

    sent = jnp.concatenate(messages, axis=0)
    got = lax.all_to_all(sent, "seq", 0, 0, tiled=True).reshape(n_seq, own_tokens, -1)
    attended = merge([got[i] for i in range(n_seq)], heads)
    attended = lax.all_gather(attended, "seq", axis=0, tiled=True)
    return lax.psum_scatter(
        jnp.dot(attended, output_weight, preferred_element_type=F32), "head", scatter_dimension=0, tiled=True
    )


def solution(mesh):
    return jax.shard_map(
        functools.partial(per_device, mesh.shape["seq"], mesh.shape["head"]),
        mesh=mesh,
        in_specs=(
            P(("groups", "seq"), "head"),
            P(("groups", "seq"), None, "head"),
            P(("groups", "seq"), None, "head"),
            P(("groups", "seq"), None, "head"),
            P("groups", "seq"),
            P("groups"),
            P("groups"),
            P("head", "seq"),
        ),
        out_specs=P(("groups", "head"), "seq"),
        check_vma=False,
    )
```

```python
import functools
import math

import jax
import jax.numpy as jnp
from jax import lax
from jax.experimental import pallas as pl
from jax.experimental.pallas import tpu as pltpu
from jax.sharding import PartitionSpec as P

HD = 128
BLOCK = 128
LANES = 128
FLOOR = -1e30
LOW_PEAK = -1e29
SCALE = math.log2(math.e) / math.sqrt(HD)
BF = jnp.bfloat16
F32 = jnp.float32


VMEM_LIMIT = 26 << 20
UNROLL = 4


def params():
    return pltpu.CompilerParams(vmem_limit_bytes=VMEM_LIMIT)


def vmem_spec():
    return pl.BlockSpec(memory_space=pltpu.VMEM)


def smem_spec():
    return pl.BlockSpec(memory_space=pltpu.SMEM)


def list_body(axis, own_tokens, shards, fin_blocks, meta_ref, lists_ref):
    here = lax.axis_index(axis)
    ctx_blocks = meta_ref.shape[1]
    owner, valid = meta_ref[meta_ref.shape[0] - 2, 0], meta_ref[meta_ref.shape[0] - 1, 0]
    end = lists_ref.shape[1] - 3
    blocks = [((here ^ k) * own_tokens) // BLOCK if here_is_first else k for here_is_first, k in shards]

    def note(i, counts):
        for at, count in enumerate(counts):
            lists_ref[at, count] = i
        return tuple(
            count + jnp.where(meta_ref[block, i] > 0, 1, 0) for count, block in zip(counts, blocks, strict=True)
        )

    counts = lax.fori_loop(0, ctx_blocks, note, (jnp.int32(0),) * len(blocks))
    for at, count in enumerate(counts):
        for i in range(UNROLL - 1):
            lists_ref[at, count + i] = ctx_blocks - 1
        lists_ref[at, end] = count
        lists_ref[at, end + 1] = jnp.where(here == owner, 1, 0)
        lists_ref[at, end + 2] = jnp.clip(valid - here * own_tokens, 0, own_tokens)


def make_lists(mask, owner, count, axis, own_tokens, shards, fin_blocks):
    shape = (len(shards), mask.shape[1] + UNROLL + 3)
    rows = [jnp.pad(x[None], ((0, 0), (0, mask.shape[1] - 1))) for x in (owner, count)]
    meta = jnp.concatenate([mask] + rows)
    return pl.pallas_call(
        functools.partial(list_body, axis, own_tokens, shards, fin_blocks),
        in_specs=[smem_spec()],
        out_specs=smem_spec(),
        out_shape=jax.ShapeDtypeStruct(shape, jnp.int32),
        cost_estimate=pl.CostEstimate(flops=4 * 1024**3, bytes_accessed=0, transcendentals=0),
        compiler_params=params(),
        name="lists",
    )(meta)


def prepare_body(at, lists_ref, cache_ref, fin_ref, own_ref, *refs):
    keys_ref, values_ref, info_ref = refs[-3:]
    width = keys_ref.shape[1]
    end = lists_ref.shape[1] - 3
    count, is_owner, limit = lists_ref[at, end], lists_ref[at, end + 1], lists_ref[at, end + 2]
    row = lax.broadcasted_iota(jnp.int32, (2 * BLOCK, 2 * BLOCK), 0)
    col = lax.broadcasted_iota(jnp.int32, (2 * BLOCK, 2 * BLOCK), 1)
    source = jnp.where(row < BLOCK, 2 * row, 2 * row - 2 * BLOCK + 1)
    pick = jnp.where(col == source, 1.0, 0.0).astype(BF)

    def take_apart(pairs, to):
        parts = jnp.dot(pick, pairs.reshape(2 * BLOCK, width), preferred_element_type=F32).astype(BF)
        rows = pl.ds(pl.multiple_of(to * BLOCK, BLOCK), BLOCK)
        keys_ref[rows] = parts[:BLOCK]
        values_ref[rows] = parts[BLOCK:]

    @pl.loop(0, (count + UNROLL - 1) // UNROLL)
    def _(j):
        for i in range(UNROLL):
            start = pl.multiple_of(lists_ref[at, j * UNROLL + i] * BLOCK, BLOCK)
            take_apart(cache_ref[pl.ds(start, BLOCK)], j * UNROLL + i)

    fin_blocks, own_rows = fin_ref.shape[0] // BLOCK, own_ref.shape[0]

    @pl.when(is_owner > 0)
    def _():
        for i in range(fin_blocks):
            take_apart(fin_ref[i * BLOCK : (i + 1) * BLOCK], count + i)

    full = count + is_owner * fin_blocks
    filler = jnp.zeros((BLOCK - own_rows, 2, width), BF)
    take_apart(jnp.concatenate([own_ref[...], filler], axis=0), full)
    unread = pl.ds(pl.multiple_of((full + 1) * BLOCK, BLOCK), BLOCK)
    keys_ref[unread] = jnp.zeros((BLOCK, width), BF)
    values_ref[unread] = jnp.zeros((BLOCK, width), BF)

    pairs = (full + 2) // 2
    lane = lax.broadcasted_iota(jnp.int32, (8, 2 * BLOCK), 1)
    edge = jnp.where(full % 2 == 0, limit, BLOCK + limit)
    info_ref[:8] = jnp.zeros((8, 2 * BLOCK), F32) + pairs.astype(F32)
    info_ref[8:] = jnp.where(lane < edge, 0.0, FLOOR)


def prepare(at, lists, cache, finished, own, after):
    rows, _, width = cache.shape
    total = rows + finished.shape[0] + UNROLL * BLOCK
    return pl.pallas_call(
        functools.partial(prepare_body, at),
        in_specs=[smem_spec(), vmem_spec(), vmem_spec(), vmem_spec()] + [pl.BlockSpec(memory_space=pl.ANY)] * len(after),
        out_specs=[vmem_spec()] * 3,
        out_shape=[jax.ShapeDtypeStruct((total, width), BF)] * 2 + [jax.ShapeDtypeStruct((16, 2 * BLOCK), F32)],
        cost_estimate=pl.CostEstimate(flops=4 * 1024**3, bytes_accessed=12 * 1024**2, transcendentals=0),
        compiler_params=params(),
        name="prepare",
    )(lists, cache, finished, own, *after)


def attend_body(geometry, *refs):
    kv, group, tokens, n = geometry
    info_ref, keys_ref, values_ref = refs[:3]
    query_refs, message_refs = refs[3 : 3 + n], refs[4 + n : 4 + 2 * n]
    scores, peaks, totals, sums = refs[4 + 2 * n :]
    rows = n * group * tokens
    pairs = jnp.max(info_ref[:8, :LANES]).astype(jnp.int32)
    stat_lane = lax.broadcasted_iota(jnp.int32, (1, LANES), 1)

    def cols(h):
        return slice(h * HD, (h + 1) * HD)

    queries = [
        jnp.concatenate([ref[:, cols(g * group + a)] for ref in query_refs for a in range(group)], axis=0)
        for g in range(kv)
    ]

    def block_rows(ref, j, g, count):
        return ref[pl.ds(pl.multiple_of(2 * BLOCK * j, 2 * BLOCK), 2 * BLOCK * count), cols(g)]

    def score(j, count, masked):
        for g in range(kv):
            top = peaks[g]
            for i in range(count):
                s = lax.dot_general(
                    queries[g], block_rows(keys_ref, j + i, g, 1), (((1,), (1,)), ((), ())), preferred_element_type=F32
                )
                if masked:
                    s = s + info_ref[8:9]
                scores[j + i, g] = s
                top = jnp.maximum(top, jnp.maximum(s[:, :BLOCK], s[:, BLOCK:]))
            peaks[g] = top

    def accumulate(j, count):
        for g in range(kv):
            total, weights = totals[g], []
            for i in range(count):
                s = scores[j + i, g]
                for half in range(2):
                    w = jnp.exp2(s[:, half * BLOCK : (half + 1) * BLOCK] * SCALE - peaks[g])
                    total = total + w
                    weights.append(w.astype(BF))
            totals[g] = total
            sums[g] += jnp.dot(
                jnp.concatenate(weights, axis=1), block_rows(values_ref, j, g, count), preferred_element_type=F32
            )

    def in_steps(total, step):
        pl.loop(0, total // 4)(lambda j: step(4 * j, 4))
        done = total // 4 * 4
        pl.when(total - done >= 2)(lambda: step(done, 2))
        pl.when(total % 2 == 1)(lambda: step(total - 1, 1))

    peaks[...] = jnp.full(peaks.shape, LOW_PEAK, F32)
    in_steps(pairs - 1, lambda j, count: score(j, count, False))
    score(pairs - 1, 1, True)

    for g in range(kv):
        peak = jnp.max(peaks[g], axis=1, keepdims=True) * SCALE
        peaks[g] = jnp.broadcast_to(peak.astype(BF).astype(F32), (rows, LANES))
    totals[...] = jnp.zeros(totals.shape, F32)
    sums[...] = jnp.zeros(sums.shape, F32)
    in_steps(pairs, accumulate)

    stats = [jnp.zeros((tokens, LANES), F32) for _ in range(n)]
    for g in range(kv):
        total = jnp.broadcast_to(jnp.sum(totals[g], axis=1, keepdims=True), (rows, LANES))
        coarse = total.astype(BF).astype(F32)
        for r in range(n):
            for a in range(group):
                h = g * group + a
                part = slice((r * group + a) * tokens, (r * group + a + 1) * tokens)
                message_refs[r][:, cols(h)] = sums[g, part].astype(BF)
                for at, value in enumerate((peaks[g, part], coarse[part], total[part] - coarse[part])):
                    stats[r] = jnp.where(stat_lane == 3 * h + at, value, stats[r])
    for r in range(n):
        message_refs[r][:, kv * group * HD :] = stats[r].astype(BF)


def attend(prepared, queries, after, kv):
    tokens, width = queries[0].shape
    n = len(queries)
    group = width // (kv * HD)
    keys, values, info = prepared
    slots = keys.shape[0] // BLOCK
    rows = n * group * tokens
    return pl.pallas_call(
        functools.partial(attend_body, (kv, group, tokens, n)),
        in_specs=[vmem_spec()] * (3 + n) + [pl.BlockSpec(memory_space=pl.ANY)],
        out_specs=[vmem_spec()] * n,
        out_shape=[jax.ShapeDtypeStruct((tokens, width + LANES), BF)] * n,
        scratch_shapes=[
            pltpu.VMEM(((slots + 1) // 2, kv, rows, 2 * BLOCK), F32),
            pltpu.VMEM((kv, rows, LANES), F32),
            pltpu.VMEM((kv, rows, LANES), F32),
            pltpu.VMEM((kv, rows, HD), F32),
        ],
        cost_estimate=pl.CostEstimate(flops=64 * 1024**2, bytes_accessed=0, transcendentals=0),
        compiler_params=params(),
        name="attend",
    )(info, keys, values, *queries, after)


def merge_body(heads, *refs):
    *parts, out_ref = refs
    loaded = [part[:, heads * HD :].astype(F32) for part in parts]
    for h in range(heads):
        peaks = [s[:, 3 * h : 3 * h + 1] for s in loaded]
        totals = [s[:, 3 * h + 1 : 3 * h + 2] + s[:, 3 * h + 2 : 3 * h + 3] for s in loaded]
        top = functools.reduce(jnp.maximum, peaks)
        factors = [jnp.exp2(p - top) for p in peaks]
        inverse = 1.0 / sum(f * t for f, t in zip(factors, totals, strict=True))
        cols = slice(h * HD, (h + 1) * HD)
        out_ref[:, cols] = sum(
            part[:, cols].astype(F32) * (f * inverse) for part, f in zip(parts, factors, strict=True)
        ).astype(BF)


def merge(parts, heads):
    tokens = parts[0].shape[0]
    return pl.pallas_call(
        functools.partial(merge_body, heads),
        in_specs=[pl.BlockSpec(memory_space=pltpu.VMEM)] * len(parts),
        out_specs=pl.BlockSpec(memory_space=pltpu.VMEM),
        out_shape=jax.ShapeDtypeStruct((tokens, heads * HD), BF),
        compiler_params=params(),
        name="merge",
    )(*parts)


def per_device(
    n_seq,
    n_head,
    segment_query,
    segment_memory,
    finished_memory,
    cache_memory,
    block_mask,
    owner_index,
    valid_count,
    output_weight,
):
    here = lax.axis_index("seq")
    own_tokens, width = segment_query.shape
    heads = width // HD
    kv = segment_memory.shape[2] // HD
    fin_blocks = finished_memory.shape[0] // BLOCK
    direct = n_seq == 4 and n_head == 4 and BLOCK == 2 * own_tokens

    def swap(value, axis, size, k):
        return lax.ppermute(value, axis, [(i, i ^ k) for i in range(size)])

    def gather_over_seq(value, between=lambda: None):
        near, far = swap(value, "seq", n_seq, 1), swap(value, "seq", n_seq, 2)
        made = between()
        if made is not None:
            far, made = lax.optimization_barrier((far, made))
        return [value, near, far, swap(far, "seq", n_seq, 1)], made

    if direct:
        shards = [(True, 2), (True, 0)]
        order = [2, 3, 1, 0]
    else:
        shards = [(False, i) for i in range(own_tokens * n_seq // BLOCK)]
    lists = make_lists(block_mask, owner_index, valid_count, "seq", own_tokens, shards, fin_blocks)

    def prepare_for(at, after):
        return prepare(at, lists, cache_memory, finished_memory, segment_memory, after)

    if direct:
        arrived, prepared = gather_over_seq(segment_query, lambda: prepare_for(0, []))
        batches = [[[arrived[k]] for k in order[:2]], [[arrived[k]] for k in order[2:]]]
    else:
        gathered = lax.all_gather(segment_query, "seq", axis=0, tiled=True)
        batches = [[[gathered[i * BLOCK : (i + 1) * BLOCK]]] for _, i in shards]
        prepared = prepare_for(0, [])

    messages, last = [], lists
    for at, of_block in enumerate(batches):
        prepared = prepared if at == 0 else prepare_for(at, [last] + of_block[0])
        for batch in of_block:
            messages += attend(prepared, batch, last, kv)
            last = messages[-1]

    if direct:
        parts = [m if k == 0 else swap(m, "seq", n_seq, k) for k, m in zip(order, messages, strict=True)]
        attended = merge([parts[i] for i in [3, 1, 0, 2]], heads)

        shards, _ = gather_over_seq(attended)
        head_at = lax.axis_index("head")
        core, side = head_at % 2, head_at // 2

        def project(rows):
            return jnp.dot(rows, output_weight, preferred_element_type=F32)

        def over_cores(pair):
            first_mine = (here ^ pair[0]) % 2 == core
            first, second = shards[pair[0]], shards[pair[1]]
            other = project(jnp.where(first_mine, second, first)).astype(BF)
            mine = project(jnp.where(first_mine, first, second))
            return mine + swap(other, "head", n_head, 1).astype(F32)

        near, far = over_cores((0, 1)), over_cores((2, 3))
        near_mine = here // 2 == side
        mine, other = jnp.where(near_mine, near, far), jnp.where(near_mine, far, near)
        return mine + swap(other.astype(BF), "head", n_head, 2).astype(F32)

    sent = jnp.concatenate(messages, axis=0)
    got = lax.all_to_all(sent, "seq", 0, 0, tiled=True).reshape(n_seq, own_tokens, -1)
    attended = merge([got[i] for i in range(n_seq)], heads)
    attended = lax.all_gather(attended, "seq", axis=0, tiled=True)
    return lax.psum_scatter(
        jnp.dot(attended, output_weight, preferred_element_type=F32), "head", scatter_dimension=0, tiled=True
    )


def solution(mesh):
    return jax.shard_map(
        functools.partial(per_device, mesh.shape["seq"], mesh.shape["head"]),
        mesh=mesh,
        in_specs=(
            P(("groups", "seq"), "head"),
            P(("groups", "seq"), None, "head"),
            P(("groups", "seq"), None, "head"),
            P(("groups", "seq"), None, "head"),
            P("groups", "seq"),
            P("groups"),
            P("groups"),
            P("head", "seq"),
        ),
        out_specs=P(("groups", "head"), "seq"),
        check_vma=False,
    )
```

```python
import functools
import math

import jax
import jax.numpy as jnp
from jax import lax
from jax.experimental import pallas as pl
from jax.experimental.pallas import tpu as pltpu
from jax.sharding import PartitionSpec as P

HD = 128
BLOCK = 128
LANES = 128
FLOOR = -1e30
LOW_PEAK = -1e29
SCALE = math.log2(math.e) / math.sqrt(HD)
BF = jnp.bfloat16
F32 = jnp.float32


VMEM_LIMIT = 26 << 20
UNROLL = 4


def params():
    return pltpu.CompilerParams(vmem_limit_bytes=VMEM_LIMIT)


def vmem_spec():
    return pl.BlockSpec(memory_space=pltpu.VMEM)


def smem_spec():
    return pl.BlockSpec(memory_space=pltpu.SMEM)


def list_body(axis, own_tokens, shards, fin_blocks, meta_ref, lists_ref):
    here = lax.axis_index(axis)
    ctx_blocks = meta_ref.shape[1]
    owner, valid = meta_ref[meta_ref.shape[0] - 2, 0], meta_ref[meta_ref.shape[0] - 1, 0]
    end = lists_ref.shape[1] - 3
    blocks = [((here ^ k) * own_tokens) // BLOCK if here_is_first else k for here_is_first, k in shards]

    def note(i, counts):
        for at, count in enumerate(counts):
            lists_ref[at, count] = i
        return tuple(
            count + jnp.where(meta_ref[block, i] > 0, 1, 0) for count, block in zip(counts, blocks, strict=True)
        )

    counts = lax.fori_loop(0, ctx_blocks, note, (jnp.int32(0),) * len(blocks))
    for at, count in enumerate(counts):
        for i in range(UNROLL - 1):
            lists_ref[at, count + i] = ctx_blocks - 1
        lists_ref[at, end] = count
        lists_ref[at, end + 1] = jnp.where(here == owner, 1, 0)
        lists_ref[at, end + 2] = jnp.clip(valid - here * own_tokens, 0, own_tokens)


def make_lists(mask, owner, count, axis, own_tokens, shards, fin_blocks):
    shape = (len(shards), mask.shape[1] + UNROLL + 3)
    rows = [jnp.pad(x[None], ((0, 0), (0, mask.shape[1] - 1))) for x in (owner, count)]
    meta = jnp.concatenate([mask] + rows)
    return pl.pallas_call(
        functools.partial(list_body, axis, own_tokens, shards, fin_blocks),
        in_specs=[smem_spec()],
        out_specs=smem_spec(),
        out_shape=jax.ShapeDtypeStruct(shape, jnp.int32),
        cost_estimate=pl.CostEstimate(flops=4 * 1024**3, bytes_accessed=0, transcendentals=0),
        compiler_params=params(),
        name="lists",
    )(meta)


def prepare_body(at, lists_ref, cache_ref, fin_ref, own_ref, *refs):
    keys_ref, values_ref, info_ref, list_ref, sem = refs[-5:]
    fetch = pltpu.make_async_copy(lists_ref, list_ref, sem)
    fetch.start()
    width = keys_ref.shape[1]
    row = lax.broadcasted_iota(jnp.int32, (2 * BLOCK, 2 * BLOCK), 0)
    col = lax.broadcasted_iota(jnp.int32, (2 * BLOCK, 2 * BLOCK), 1)
    source = jnp.where(row < BLOCK, 2 * row, 2 * row - 2 * BLOCK + 1)
    pick = jnp.where(col == source, 1.0, 0.0).astype(BF)

    def take_apart(pairs):
        parts = jnp.dot(pick, pairs.reshape(2 * BLOCK, width), preferred_element_type=F32).astype(BF)
        return parts[:BLOCK], parts[BLOCK:]

    def put(parts, to):
        rows = pl.ds(pl.multiple_of(to * BLOCK, BLOCK), BLOCK)
        keys_ref[rows], values_ref[rows] = parts

    fin_blocks, own_rows = fin_ref.shape[0] // BLOCK, own_ref.shape[0]
    filler = jnp.zeros((BLOCK - own_rows, 2, width), BF)
    own = take_apart(jnp.concatenate([own_ref[...], filler], axis=0))
    finished = [take_apart(fin_ref[i * BLOCK : (i + 1) * BLOCK]) for i in range(fin_blocks)]
    fetch.wait()
    end = list_ref.shape[1] - 3
    count, is_owner, limit = list_ref[at, end], list_ref[at, end + 1], list_ref[at, end + 2]
    full = count + is_owner * fin_blocks

    @pl.loop(0, (count + UNROLL - 1) // UNROLL)
    def _(j):
        for i in range(UNROLL):
            start = pl.multiple_of(list_ref[at, j * UNROLL + i] * BLOCK, BLOCK)
            put(take_apart(cache_ref[pl.ds(start, BLOCK)]), j * UNROLL + i)

    for i in range(fin_blocks):
        put(finished[i], count + i)
    put(own, full)
    zeros = jnp.zeros((BLOCK, width), BF)
    put((zeros, zeros), full + 1)

    pairs = (full + 2) // 2
    lane = lax.broadcasted_iota(jnp.int32, (8, 2 * BLOCK), 1)
    edge = jnp.where(full % 2 == 0, limit, BLOCK + limit)
    info_ref[:8] = jnp.zeros((8, 2 * BLOCK), F32) + pairs.astype(F32)
    info_ref[8:] = jnp.where(lane < edge, 0.0, FLOOR)


def prepare(at, lists, cache, finished, own, after):
    rows, _, width = cache.shape
    total = rows + finished.shape[0] + UNROLL * BLOCK
    return pl.pallas_call(
        functools.partial(prepare_body, at),
        in_specs=[vmem_spec()] * 4 + [pl.BlockSpec(memory_space=pl.ANY)] * len(after),
        out_specs=[vmem_spec()] * 3,
        out_shape=[jax.ShapeDtypeStruct((total, width), BF)] * 2 + [jax.ShapeDtypeStruct((16, 2 * BLOCK), F32)],
        scratch_shapes=[pltpu.SMEM(lists.shape, jnp.int32), pltpu.SemaphoreType.DMA],
        cost_estimate=pl.CostEstimate(flops=4 * 1024**3, bytes_accessed=12 * 1024**2, transcendentals=0),
        compiler_params=params(),
        name="prepare",
    )(lists, cache, finished, own, *after)


def attend_body(geometry, *refs):
    kv, group, tokens, n = geometry
    info_ref, keys_ref, values_ref = refs[:3]
    query_refs, message_refs = refs[3 : 3 + n], refs[4 + n : 4 + 2 * n]
    scores, peaks, totals, sums = refs[4 + 2 * n :]
    rows = n * group * tokens
    pairs = jnp.max(info_ref[:8, :LANES]).astype(jnp.int32)
    stat_lane = lax.broadcasted_iota(jnp.int32, (1, LANES), 1)

    def cols(h):
        return slice(h * HD, (h + 1) * HD)

    queries = [
        jnp.concatenate([ref[:, cols(g * group + a)] for ref in query_refs for a in range(group)], axis=0)
        for g in range(kv)
    ]

    def block_rows(ref, j, g, count):
        return ref[pl.ds(pl.multiple_of(2 * BLOCK * j, 2 * BLOCK), 2 * BLOCK * count), cols(g)]

    def score(j, count, masked):
        for g in range(kv):
            top = peaks[g]
            for i in range(count):
                s = lax.dot_general(
                    queries[g], block_rows(keys_ref, j + i, g, 1), (((1,), (1,)), ((), ())), preferred_element_type=F32
                )
                if masked:
                    s = s + info_ref[8:9]
                scores[j + i, g] = s
                top = jnp.maximum(top, jnp.maximum(s[:, :BLOCK], s[:, BLOCK:]))
            peaks[g] = top

    def accumulate(j, count):
        for g in range(kv):
            total, weights = totals[g], []
            for i in range(count):
                s = scores[j + i, g]
                for half in range(2):
                    w = jnp.exp2(s[:, half * BLOCK : (half + 1) * BLOCK] * SCALE - peaks[g])
                    total = total + w
                    weights.append(w.astype(BF))
            totals[g] = total
            sums[g] += jnp.dot(
                jnp.concatenate(weights, axis=1), block_rows(values_ref, j, g, count), preferred_element_type=F32
            )

    def in_steps(total, step):
        pl.loop(0, total // 8)(lambda j: step(8 * j, 8))
        pl.when(total % 8 >= 4)(lambda: step(total // 8 * 8, 4))
        done = total // 4 * 4
        pl.when(total - done >= 2)(lambda: step(done, 2))
        pl.when(total % 2 == 1)(lambda: step(total - 1, 1))

    peaks[...] = jnp.full(peaks.shape, LOW_PEAK, F32)
    in_steps(pairs - 1, lambda j, count: score(j, count, False))
    score(pairs - 1, 1, True)

    for g in range(kv):
        peak = jnp.max(peaks[g], axis=1, keepdims=True) * SCALE
        peaks[g] = jnp.broadcast_to(peak.astype(BF).astype(F32), (rows, LANES))
    totals[...] = jnp.zeros(totals.shape, F32)
    sums[...] = jnp.zeros(sums.shape, F32)
    in_steps(pairs, accumulate)

    stats = [jnp.zeros((tokens, LANES), F32) for _ in range(n)]
    for g in range(kv):
        total = jnp.broadcast_to(jnp.sum(totals[g], axis=1, keepdims=True), (rows, LANES))
        coarse = total.astype(BF).astype(F32)
        for r in range(n):
            for a in range(group):
                h = g * group + a
                part = slice((r * group + a) * tokens, (r * group + a + 1) * tokens)
                message_refs[r][:, cols(h)] = sums[g, part].astype(BF)
                for at, value in enumerate((peaks[g, part], coarse[part], total[part] - coarse[part])):
                    stats[r] = jnp.where(stat_lane == 3 * h + at, value, stats[r])
    for r in range(n):
        message_refs[r][:, kv * group * HD :] = stats[r].astype(BF)


def attend(prepared, queries, after, kv):
    tokens, width = queries[0].shape
    n = len(queries)
    group = width // (kv * HD)
    keys, values, info = prepared
    slots = keys.shape[0] // BLOCK
    rows = n * group * tokens
    return pl.pallas_call(
        functools.partial(attend_body, (kv, group, tokens, n)),
        in_specs=[vmem_spec()] * (3 + n) + [pl.BlockSpec(memory_space=pl.ANY)],
        out_specs=[vmem_spec()] * n,
        out_shape=[jax.ShapeDtypeStruct((tokens, width + LANES), BF)] * n,
        scratch_shapes=[
            pltpu.VMEM(((slots + 1) // 2, kv, rows, 2 * BLOCK), F32),
            pltpu.VMEM((kv, rows, LANES), F32),
            pltpu.VMEM((kv, rows, LANES), F32),
            pltpu.VMEM((kv, rows, HD), F32),
        ],
        cost_estimate=pl.CostEstimate(flops=64 * 1024**2, bytes_accessed=0, transcendentals=0),
        compiler_params=params(),
        name="attend",
    )(info, keys, values, *queries, after)


def merge_body(heads, *refs):
    *parts, out_ref = refs
    loaded = [part[:, heads * HD :].astype(F32) for part in parts]
    for h in range(heads):
        peaks = [s[:, 3 * h : 3 * h + 1] for s in loaded]
        totals = [s[:, 3 * h + 1 : 3 * h + 2] + s[:, 3 * h + 2 : 3 * h + 3] for s in loaded]
        top = functools.reduce(jnp.maximum, peaks)
        factors = [jnp.exp2(p - top) for p in peaks]
        inverse = 1.0 / sum(f * t for f, t in zip(factors, totals, strict=True))
        cols = slice(h * HD, (h + 1) * HD)
        out_ref[:, cols] = sum(
            part[:, cols].astype(F32) * (f * inverse) for part, f in zip(parts, factors, strict=True)
        ).astype(BF)


def merge(parts, heads):
    tokens = parts[0].shape[0]
    return pl.pallas_call(
        functools.partial(merge_body, heads),
        in_specs=[pl.BlockSpec(memory_space=pltpu.VMEM)] * len(parts),
        out_specs=pl.BlockSpec(memory_space=pltpu.VMEM),
        out_shape=jax.ShapeDtypeStruct((tokens, heads * HD), BF),
        compiler_params=params(),
        name="merge",
    )(*parts)


def per_device(
    n_seq,
    n_head,
    segment_query,
    segment_memory,
    finished_memory,
    cache_memory,
    block_mask,
    owner_index,
    valid_count,
    output_weight,
):
    here = lax.axis_index("seq")
    own_tokens, width = segment_query.shape
    heads = width // HD
    kv = segment_memory.shape[2] // HD
    fin_blocks = finished_memory.shape[0] // BLOCK
    direct = n_seq == 4 and n_head == 4 and BLOCK == 2 * own_tokens

    def swap(value, axis, size, k):
        return lax.ppermute(value, axis, [(i, i ^ k) for i in range(size)])

    def gather_over_seq(value, between=lambda: None):
        near, far = swap(value, "seq", n_seq, 1), swap(value, "seq", n_seq, 2)
        made = between()
        if made is not None:
            far, made = lax.optimization_barrier((far, made))
        return [value, near, far, swap(far, "seq", n_seq, 1)], made

    if direct:
        shards = [(True, 2), (True, 0)]
        order = [2, 3, 1, 0]
    else:
        shards = [(False, i) for i in range(own_tokens * n_seq // BLOCK)]
    lists = make_lists(block_mask, owner_index, valid_count, "seq", own_tokens, shards, fin_blocks)

    def prepare_for(at, after):
        return prepare(at, lists, cache_memory, finished_memory, segment_memory, after)

    if direct:
        arrived, prepared = gather_over_seq(segment_query, lambda: prepare_for(0, []))
        batches = [[[arrived[k]] for k in order[:2]], [[arrived[k]] for k in order[2:]]]
    else:
        gathered = lax.all_gather(segment_query, "seq", axis=0, tiled=True)
        batches = [[[gathered[i * BLOCK : (i + 1) * BLOCK]]] for _, i in shards]
        prepared = prepare_for(0, [])

    messages, last = [], lists
    for at, of_block in enumerate(batches):
        prepared = prepared if at == 0 else prepare_for(at, [last] + of_block[0])
        for batch in of_block:
            messages += attend(prepared, batch, last, kv)
            last = messages[-1]

    if direct:
        parts = [m if k == 0 else swap(m, "seq", n_seq, k) for k, m in zip(order, messages, strict=True)]
        attended = merge([parts[i] for i in [3, 1, 0, 2]], heads)

        shards, _ = gather_over_seq(attended)
        head_at = lax.axis_index("head")
        core, side = head_at % 2, head_at // 2

        def project(rows):
            return jnp.dot(rows, output_weight, preferred_element_type=F32)

        def over_cores(pair):
            first_mine = (here ^ pair[0]) % 2 == core
            first, second = shards[pair[0]], shards[pair[1]]
            other = project(jnp.where(first_mine, second, first)).astype(BF)
            mine = project(jnp.where(first_mine, first, second))
            return mine + swap(other, "head", n_head, 1).astype(F32)

        near, far = over_cores((0, 1)), over_cores((2, 3))
        near_mine = here // 2 == side
        mine, other = jnp.where(near_mine, near, far), jnp.where(near_mine, far, near)
        return mine + swap(other.astype(BF), "head", n_head, 2).astype(F32)

    sent = jnp.concatenate(messages, axis=0)
    got = lax.all_to_all(sent, "seq", 0, 0, tiled=True).reshape(n_seq, own_tokens, -1)
    attended = merge([got[i] for i in range(n_seq)], heads)
    attended = lax.all_gather(attended, "seq", axis=0, tiled=True)
    return lax.psum_scatter(
        jnp.dot(attended, output_weight, preferred_element_type=F32), "head", scatter_dimension=0, tiled=True
    )


def solution(mesh):
    return jax.shard_map(
        functools.partial(per_device, mesh.shape["seq"], mesh.shape["head"]),
        mesh=mesh,
        in_specs=(
            P(("groups", "seq"), "head"),
            P(("groups", "seq"), None, "head"),
            P(("groups", "seq"), None, "head"),
            P(("groups", "seq"), None, "head"),
            P("groups", "seq"),
            P("groups"),
            P("groups"),
            P("head", "seq"),
        ),
        out_specs=P(("groups", "head"), "seq"),
        check_vma=False,
    )
```

```python
import functools
import math

import jax
import jax.numpy as jnp
from jax import lax
from jax.experimental import pallas as pl
from jax.experimental.pallas import tpu as pltpu
from jax.sharding import PartitionSpec as P

HD = 128
BLOCK = 128
LANES = 128
FLOOR = -1e30
LOW_PEAK = -1e29
SCALE = math.log2(math.e) / math.sqrt(HD)
BF = jnp.bfloat16
F32 = jnp.float32


VMEM_LIMIT = 26 << 20
UNROLL = 4


def params():
    return pltpu.CompilerParams(vmem_limit_bytes=VMEM_LIMIT)


def vmem_spec():
    return pl.BlockSpec(memory_space=pltpu.VMEM)


def smem_spec():
    return pl.BlockSpec(memory_space=pltpu.SMEM)


def list_body(axis, own_tokens, shards, fin_blocks, meta_ref, lists_ref):
    here = lax.axis_index(axis)
    ctx_blocks = meta_ref.shape[1]
    owner, valid = meta_ref[meta_ref.shape[0] - 2, 0], meta_ref[meta_ref.shape[0] - 1, 0]
    end = lists_ref.shape[1] - 3
    blocks = [((here ^ k) * own_tokens) // BLOCK if here_is_first else k for here_is_first, k in shards]

    def note(i, counts):
        for at, count in enumerate(counts):
            lists_ref[at, count] = i
        return tuple(
            count + jnp.where(meta_ref[block, i] > 0, 1, 0) for count, block in zip(counts, blocks, strict=True)
        )

    counts = lax.fori_loop(0, ctx_blocks, note, (jnp.int32(0),) * len(blocks))
    for at, count in enumerate(counts):
        for i in range(UNROLL - 1):
            lists_ref[at, count + i] = ctx_blocks - 1
        lists_ref[at, end] = count
        lists_ref[at, end + 1] = jnp.where(here == owner, 1, 0)
        lists_ref[at, end + 2] = jnp.clip(valid - here * own_tokens, 0, own_tokens)


def make_lists(mask, owner, count, axis, own_tokens, shards, fin_blocks):
    shape = (len(shards), mask.shape[1] + UNROLL + 3)
    rows = [jnp.pad(x[None], ((0, 0), (0, mask.shape[1] - 1))) for x in (owner, count)]
    meta = jnp.concatenate([mask] + rows)
    return pl.pallas_call(
        functools.partial(list_body, axis, own_tokens, shards, fin_blocks),
        in_specs=[smem_spec()],
        out_specs=smem_spec(),
        out_shape=jax.ShapeDtypeStruct(shape, jnp.int32),
        cost_estimate=pl.CostEstimate(flops=4 * 1024**3, bytes_accessed=0, transcendentals=0),
        compiler_params=params(),
        name="lists",
    )(meta)


def prepare_body(at, lists_ref, cache_ref, fin_ref, own_ref, *refs):
    keys_ref, values_ref, info_ref, list_ref, sem = refs[-5:]
    fetch = pltpu.make_async_copy(lists_ref, list_ref, sem)
    fetch.start()
    width = keys_ref.shape[1]
    row = lax.broadcasted_iota(jnp.int32, (2 * BLOCK, 2 * BLOCK), 0)
    col = lax.broadcasted_iota(jnp.int32, (2 * BLOCK, 2 * BLOCK), 1)
    source = jnp.where(row < BLOCK, 2 * row, 2 * row - 2 * BLOCK + 1)
    pick = jnp.where(col == source, 1.0, 0.0).astype(BF)

    def take_apart(pairs):
        parts = jnp.dot(pick, pairs.reshape(2 * BLOCK, width), preferred_element_type=F32).astype(BF)
        return parts[:BLOCK], parts[BLOCK:]

    def put(parts, to):
        rows = pl.ds(pl.multiple_of(to * BLOCK, BLOCK), BLOCK)
        keys_ref[rows], values_ref[rows] = parts

    fin_blocks, own_rows = fin_ref.shape[0] // BLOCK, own_ref.shape[0]
    filler = jnp.zeros((BLOCK - own_rows, 2, width), BF)
    own = take_apart(jnp.concatenate([own_ref[...], filler], axis=0))
    finished = [take_apart(fin_ref[i * BLOCK : (i + 1) * BLOCK]) for i in range(fin_blocks)]
    fetch.wait()
    end = list_ref.shape[1] - 3
    count, is_owner, limit = list_ref[at, end], list_ref[at, end + 1], list_ref[at, end + 2]
    full = count + is_owner * fin_blocks

    @pl.loop(0, (count + UNROLL - 1) // UNROLL)
    def _(j):
        for i in range(UNROLL):
            start = pl.multiple_of(list_ref[at, j * UNROLL + i] * BLOCK, BLOCK)
            put(take_apart(cache_ref[pl.ds(start, BLOCK)]), j * UNROLL + i)

    for i in range(fin_blocks):
        put(finished[i], count + i)
    put(own, full)
    zeros = jnp.zeros((BLOCK, width), BF)
    put((zeros, zeros), full + 1)

    pairs = (full + 2) // 2
    lane = lax.broadcasted_iota(jnp.int32, (8, 2 * BLOCK), 1)
    edge = jnp.where(full % 2 == 0, limit, BLOCK + limit)
    info_ref[:8] = jnp.zeros((8, 2 * BLOCK), F32) + pairs.astype(F32)
    info_ref[8:] = jnp.where(lane < edge, 0.0, FLOOR)


def prepare(at, lists, cache, finished, own, after):
    rows, _, width = cache.shape
    total = rows + finished.shape[0] + UNROLL * BLOCK
    return pl.pallas_call(
        functools.partial(prepare_body, at),
        in_specs=[vmem_spec()] * 4 + [pl.BlockSpec(memory_space=pl.ANY)] * len(after),
        out_specs=[vmem_spec()] * 3,
        out_shape=[jax.ShapeDtypeStruct((total, width), BF)] * 2 + [jax.ShapeDtypeStruct((16, 2 * BLOCK), F32)],
        scratch_shapes=[pltpu.SMEM(lists.shape, jnp.int32), pltpu.SemaphoreType.DMA],
        cost_estimate=pl.CostEstimate(flops=4 * 1024**3, bytes_accessed=12 * 1024**2, transcendentals=0),
        compiler_params=params(),
        name="prepare",
    )(lists, cache, finished, own, *after)


def attend_body(geometry, *refs):
    kv, group, tokens, n = geometry
    info_ref, keys_ref, values_ref = refs[:3]
    query_refs, message_refs = refs[3 : 3 + n], refs[4 + n : 4 + 2 * n]
    scores, peaks, totals, sums = refs[4 + 2 * n :]
    rows = n * group * tokens
    pairs = jnp.max(info_ref[:8, :LANES]).astype(jnp.int32)
    stat_lane = lax.broadcasted_iota(jnp.int32, (1, LANES), 1)

    def cols(h):
        return slice(h * HD, (h + 1) * HD)

    queries = [
        jnp.concatenate([ref[:, cols(g * group + a)] for ref in query_refs for a in range(group)], axis=0)
        for g in range(kv)
    ]

    def block_rows(ref, j, g, count):
        return ref[pl.ds(pl.multiple_of(2 * BLOCK * j, 2 * BLOCK), 2 * BLOCK * count), cols(g)]

    def score(j, count, masked):
        for g in range(kv):
            top = peaks[g]
            for i in range(count):
                s = lax.dot_general(
                    queries[g], block_rows(keys_ref, j + i, g, 1), (((1,), (1,)), ((), ())), preferred_element_type=F32
                )
                if masked:
                    s = s + info_ref[8:9]
                scores[j + i, g] = s
                top = jnp.maximum(top, jnp.maximum(s[:, :BLOCK], s[:, BLOCK:]))
            peaks[g] = top

    def accumulate(j, count):
        for g in range(kv):
            total, weights = totals[g], []
            for i in range(count):
                s = scores[j + i, g]
                for half in range(2):
                    w = jnp.exp2(s[:, half * BLOCK : (half + 1) * BLOCK] * SCALE - peaks[g])
                    total = total + w
                    weights.append(w.astype(BF))
            totals[g] = total
            sums[g] += jnp.dot(
                jnp.concatenate(weights, axis=1), block_rows(values_ref, j, g, count), preferred_element_type=F32
            )

    def in_steps(total, step):
        pl.loop(0, total // 8)(lambda j: step(8 * j, 8))
        pl.when(total % 8 >= 4)(lambda: step(total // 8 * 8, 4))
        done = total // 4 * 4
        pl.when(total - done >= 2)(lambda: step(done, 2))
        pl.when(total % 2 == 1)(lambda: step(total - 1, 1))

    peaks[...] = jnp.full(peaks.shape, LOW_PEAK, F32)
    in_steps(pairs - 1, lambda j, count: score(j, count, False))
    score(pairs - 1, 1, True)

    for g in range(kv):
        peak = jnp.max(peaks[g], axis=1, keepdims=True) * SCALE
        peaks[g] = jnp.broadcast_to(peak.astype(BF).astype(F32), (rows, LANES))
    totals[...] = jnp.zeros(totals.shape, F32)
    sums[...] = jnp.zeros(sums.shape, F32)
    in_steps(pairs, accumulate)

    stats = [jnp.zeros((tokens, LANES), F32) for _ in range(n)]
    for g in range(kv):
        total = jnp.broadcast_to(jnp.sum(totals[g], axis=1, keepdims=True), (rows, LANES))
        coarse = total.astype(BF).astype(F32)
        for r in range(n):
            for a in range(group):
                h = g * group + a
                part = slice((r * group + a) * tokens, (r * group + a + 1) * tokens)
                message_refs[r][:, cols(h)] = sums[g, part].astype(BF)
                for at, value in enumerate((peaks[g, part], coarse[part], total[part] - coarse[part])):
                    stats[r] = jnp.where(stat_lane == 3 * h + at, value, stats[r])
    for r in range(n):
        message_refs[r][:, kv * group * HD :] = stats[r].astype(BF)


def attend(prepared, queries, after, kv):
    tokens, width = queries[0].shape
    n = len(queries)
    group = width // (kv * HD)
    keys, values, info = prepared
    slots = keys.shape[0] // BLOCK
    rows = n * group * tokens
    return pl.pallas_call(
        functools.partial(attend_body, (kv, group, tokens, n)),
        in_specs=[vmem_spec()] * (3 + n) + [pl.BlockSpec(memory_space=pl.ANY)],
        out_specs=[vmem_spec()] * n,
        out_shape=[jax.ShapeDtypeStruct((tokens, width + LANES), BF)] * n,
        scratch_shapes=[
            pltpu.VMEM(((slots + 1) // 2, kv, rows, 2 * BLOCK), F32),
            pltpu.VMEM((kv, rows, LANES), F32),
            pltpu.VMEM((kv, rows, LANES), F32),
            pltpu.VMEM((kv, rows, HD), F32),
        ],
        cost_estimate=pl.CostEstimate(flops=64 * 1024**2, bytes_accessed=0, transcendentals=0),
        compiler_params=params(),
        name="attend",
    )(info, keys, values, *queries, after)


def merge_body(heads, *refs):
    *parts, out_ref = refs
    loaded = [part[:, heads * HD :].astype(F32) for part in parts]
    for h in range(heads):
        peaks = [s[:, 3 * h : 3 * h + 1] for s in loaded]
        totals = [s[:, 3 * h + 1 : 3 * h + 2] + s[:, 3 * h + 2 : 3 * h + 3] for s in loaded]
        top = functools.reduce(jnp.maximum, peaks)
        factors = [jnp.exp2(p - top) for p in peaks]
        inverse = 1.0 / sum(f * t for f, t in zip(factors, totals, strict=True))
        cols = slice(h * HD, (h + 1) * HD)
        out_ref[:, cols] = sum(
            part[:, cols].astype(F32) * (f * inverse) for part, f in zip(parts, factors, strict=True)
        ).astype(BF)


def merge(parts, heads):
    tokens = parts[0].shape[0]
    return pl.pallas_call(
        functools.partial(merge_body, heads),
        in_specs=[pl.BlockSpec(memory_space=pltpu.VMEM)] * len(parts),
        out_specs=pl.BlockSpec(memory_space=pltpu.VMEM),
        out_shape=jax.ShapeDtypeStruct((tokens, heads * HD), BF),
        compiler_params=params(),
        name="merge",
    )(*parts)


def per_device(
    n_seq,
    n_head,
    segment_query,
    segment_memory,
    finished_memory,
    cache_memory,
    block_mask,
    owner_index,
    valid_count,
    output_weight,
):
    here = lax.axis_index("seq")
    own_tokens, width = segment_query.shape
    heads = width // HD
    kv = segment_memory.shape[2] // HD
    fin_blocks = finished_memory.shape[0] // BLOCK
    direct = n_seq == 4 and n_head == 4 and BLOCK == 2 * own_tokens

    def swap(value, axis, size, k):
        return lax.ppermute(value, axis, [(i, i ^ k) for i in range(size)])

    def gather_over_seq(value, between=lambda: None):
        near, far = swap(value, "seq", n_seq, 1), swap(value, "seq", n_seq, 2)
        made = between()
        if made is not None:
            far, made = lax.optimization_barrier((far, made))
        return [value, near, far, swap(far, "seq", n_seq, 1)], made

    if direct:
        shards = [(True, 2), (True, 0)]
        order = [2, 3, 1, 0]
    else:
        shards = [(False, i) for i in range(own_tokens * n_seq // BLOCK)]
    lists = make_lists(block_mask, owner_index, valid_count, "seq", own_tokens, shards, fin_blocks)

    def prepare_for(at, after):
        return prepare(at, lists, cache_memory, finished_memory, segment_memory, after)

    if direct:
        arrived, prepared = gather_over_seq(segment_query, lambda: prepare_for(0, []))
        batches = [[[arrived[k]] for k in order[:2]], [[arrived[k]] for k in order[2:]]]
    else:
        gathered = lax.all_gather(segment_query, "seq", axis=0, tiled=True)
        batches = [[[gathered[i * BLOCK : (i + 1) * BLOCK]]] for _, i in shards]
        prepared = prepare_for(0, [])

    messages, last = [], lists
    for at, of_block in enumerate(batches):
        prepared = prepared if at == 0 else prepare_for(at, [last] + of_block[0])
        for batch in of_block:
            messages += attend(prepared, batch, last, kv)
            last = messages[-1]

    if direct:
        parts = [m if k == 0 else swap(m, "seq", n_seq, k) for k, m in zip(order, messages, strict=True)]
        attended = merge([parts[i] for i in [3, 1, 0, 2]], heads)

        shards, _ = gather_over_seq(attended)
        head_at = lax.axis_index("head")
        core, side = head_at % 2, head_at // 2

        def project(rows):
            return jnp.dot(rows, output_weight, preferred_element_type=F32)

        def over_cores(pair):
            first_mine = (here ^ pair[0]) % 2 == core
            first, second = shards[pair[0]], shards[pair[1]]
            other = project(jnp.where(first_mine, second, first)).astype(BF)
            mine = project(jnp.where(first_mine, first, second))
            if pair[0] == 0:
                other, mine = lax.optimization_barrier((other, mine))
            received = swap(other, "head", n_head, 1)
            if pair[0] == 2:
                received, mine = lax.optimization_barrier((received, mine))
            return mine + received.astype(F32)

        near, far = over_cores((0, 1)), over_cores((2, 3))
        near_mine = here // 2 == side
        mine, other = jnp.where(near_mine, near, far), jnp.where(near_mine, far, near)
        return mine + swap(other.astype(BF), "head", n_head, 2).astype(F32)

    sent = jnp.concatenate(messages, axis=0)
    got = lax.all_to_all(sent, "seq", 0, 0, tiled=True).reshape(n_seq, own_tokens, -1)
    attended = merge([got[i] for i in range(n_seq)], heads)
    attended = lax.all_gather(attended, "seq", axis=0, tiled=True)
    return lax.psum_scatter(
        jnp.dot(attended, output_weight, preferred_element_type=F32), "head", scatter_dimension=0, tiled=True
    )


def solution(mesh):
    return jax.shard_map(
        functools.partial(per_device, mesh.shape["seq"], mesh.shape["head"]),
        mesh=mesh,
        in_specs=(
            P(("groups", "seq"), "head"),
            P(("groups", "seq"), None, "head"),
            P(("groups", "seq"), None, "head"),
            P(("groups", "seq"), None, "head"),
            P("groups", "seq"),
            P("groups"),
            P("groups"),
            P("head", "seq"),
        ),
        out_specs=P(("groups", "head"), "seq"),
        check_vma=False,
    )
```

```python
import functools
import math

import jax
import jax.numpy as jnp
from jax import lax
from jax.experimental import pallas as pl
from jax.experimental.pallas import tpu as pltpu
from jax.sharding import PartitionSpec as P

HD = 128
BLOCK = 128
LANES = 128
FLOOR = -1e30
LOW_PEAK = -1e29
SCALE = math.log2(math.e) / math.sqrt(HD)
BF = jnp.bfloat16
F32 = jnp.float32


VMEM_LIMIT = 26 << 20
UNROLL = 6


def params():
    return pltpu.CompilerParams(vmem_limit_bytes=VMEM_LIMIT)


def vmem_spec():
    return pl.BlockSpec(memory_space=pltpu.VMEM)


def smem_spec():
    return pl.BlockSpec(memory_space=pltpu.SMEM)


def list_body(axis, own_tokens, shards, fin_blocks, meta_ref, lists_ref):
    here = lax.axis_index(axis)
    ctx_blocks = meta_ref.shape[1]
    owner, valid = meta_ref[meta_ref.shape[0] - 2, 0], meta_ref[meta_ref.shape[0] - 1, 0]
    end = lists_ref.shape[1] - 3
    blocks = [((here ^ k) * own_tokens) // BLOCK if here_is_first else k for here_is_first, k in shards]

    def note(i, counts):
        for at, count in enumerate(counts):
            lists_ref[at, count] = i
        return tuple(
            count + jnp.where(meta_ref[block, i] > 0, 1, 0) for count, block in zip(counts, blocks, strict=True)
        )

    counts = lax.fori_loop(0, ctx_blocks, note, (jnp.int32(0),) * len(blocks))
    for at, count in enumerate(counts):
        for i in range(UNROLL - 1):
            lists_ref[at, count + i] = ctx_blocks - 1
        lists_ref[at, end] = count
        lists_ref[at, end + 1] = jnp.where(here == owner, 1, 0)
        lists_ref[at, end + 2] = jnp.clip(valid - here * own_tokens, 0, own_tokens)


def make_lists(mask, owner, count, axis, own_tokens, shards, fin_blocks):
    shape = (len(shards), mask.shape[1] + UNROLL + 3)
    rows = [jnp.pad(x[None], ((0, 0), (0, mask.shape[1] - 1))) for x in (owner, count)]
    meta = jnp.concatenate([mask] + rows)
    return pl.pallas_call(
        functools.partial(list_body, axis, own_tokens, shards, fin_blocks),
        in_specs=[smem_spec()],
        out_specs=smem_spec(),
        out_shape=jax.ShapeDtypeStruct(shape, jnp.int32),
        cost_estimate=pl.CostEstimate(flops=4 * 1024**3, bytes_accessed=0, transcendentals=0),
        compiler_params=params(),
        name="lists",
    )(meta)


def prepare_body(at, lists_ref, cache_ref, fin_ref, own_ref, *refs):
    keys_ref, values_ref, info_ref, list_ref, sem = refs[-5:]
    fetch = pltpu.make_async_copy(lists_ref, list_ref, sem)
    fetch.start()
    width = keys_ref.shape[1]
    row = lax.broadcasted_iota(jnp.int32, (2 * BLOCK, 2 * BLOCK), 0)
    col = lax.broadcasted_iota(jnp.int32, (2 * BLOCK, 2 * BLOCK), 1)
    source = jnp.where(row < BLOCK, 2 * row, 2 * row - 2 * BLOCK + 1)
    pick = jnp.where(col == source, 1.0, 0.0).astype(BF)

    def take_apart(pairs):
        parts = jnp.dot(pick, pairs.reshape(2 * BLOCK, width), preferred_element_type=F32).astype(BF)
        return parts[:BLOCK], parts[BLOCK:]

    def put(parts, to):
        rows = pl.ds(pl.multiple_of(to * BLOCK, BLOCK), BLOCK)
        keys_ref[rows], values_ref[rows] = parts

    fin_blocks, own_rows = fin_ref.shape[0] // BLOCK, own_ref.shape[0]
    filler = jnp.zeros((BLOCK - own_rows, 2, width), BF)
    own = take_apart(jnp.concatenate([own_ref[...], filler], axis=0))
    finished = [take_apart(fin_ref[i * BLOCK : (i + 1) * BLOCK]) for i in range(fin_blocks)]
    fetch.wait()
    end = list_ref.shape[1] - 3
    count, is_owner, limit = list_ref[at, end], list_ref[at, end + 1], list_ref[at, end + 2]
    full = count + is_owner * fin_blocks

    @pl.loop(0, (count + UNROLL - 1) // UNROLL)
    def _(j):
        for i in range(UNROLL):
            start = pl.multiple_of(list_ref[at, j * UNROLL + i] * BLOCK, BLOCK)
            put(take_apart(cache_ref[pl.ds(start, BLOCK)]), j * UNROLL + i)

    for i in range(fin_blocks):
        put(finished[i], count + i)
    put(own, full)
    zeros = jnp.zeros((BLOCK, width), BF)
    put((zeros, zeros), full + 1)

    pairs = (full + 2) // 2
    lane = lax.broadcasted_iota(jnp.int32, (8, 2 * BLOCK), 1)
    edge = jnp.where(full % 2 == 0, limit, BLOCK + limit)
    info_ref[:8] = jnp.zeros((8, 2 * BLOCK), F32) + pairs.astype(F32)
    info_ref[8:] = jnp.where(lane < edge, 0.0, FLOOR)


def prepare(at, lists, cache, finished, own, after):
    rows, _, width = cache.shape
    total = rows + finished.shape[0] + UNROLL * BLOCK
    return pl.pallas_call(
        functools.partial(prepare_body, at),
        in_specs=[vmem_spec()] * 4 + [pl.BlockSpec(memory_space=pl.ANY)] * len(after),
        out_specs=[vmem_spec()] * 3,
        out_shape=[jax.ShapeDtypeStruct((total, width), BF)] * 2 + [jax.ShapeDtypeStruct((16, 2 * BLOCK), F32)],
        scratch_shapes=[pltpu.SMEM(lists.shape, jnp.int32), pltpu.SemaphoreType.DMA],
        cost_estimate=pl.CostEstimate(flops=4 * 1024**3, bytes_accessed=12 * 1024**2, transcendentals=0),
        compiler_params=params(),
        name="prepare",
    )(lists, cache, finished, own, *after)


def attend_body(geometry, *refs):
    kv, group, tokens, n = geometry
    info_ref, keys_ref, values_ref = refs[:3]
    query_refs, message_refs = refs[3 : 3 + n], refs[4 + n : 4 + 2 * n]
    scores, peaks, totals, sums = refs[4 + 2 * n :]
    rows = n * group * tokens
    pairs = jnp.max(info_ref[:8, :LANES]).astype(jnp.int32)
    stat_lane = lax.broadcasted_iota(jnp.int32, (1, LANES), 1)

    def cols(h):
        return slice(h * HD, (h + 1) * HD)

    queries = [
        jnp.concatenate([ref[:, cols(g * group + a)] for ref in query_refs for a in range(group)], axis=0)
        for g in range(kv)
    ]

    def block_rows(ref, j, g, count):
        return ref[pl.ds(pl.multiple_of(2 * BLOCK * j, 2 * BLOCK), 2 * BLOCK * count), cols(g)]

    def score(j, count, masked):
        for g in range(kv):
            top = peaks[g]
            for i in range(count):
                s = lax.dot_general(
                    queries[g], block_rows(keys_ref, j + i, g, 1), (((1,), (1,)), ((), ())), preferred_element_type=F32
                )
                if masked:
                    s = s + info_ref[8:9]
                scores[j + i, g] = s
                top = jnp.maximum(top, jnp.maximum(s[:, :BLOCK], s[:, BLOCK:]))
            peaks[g] = top

    def accumulate(j, count):
        for g in range(kv):
            total, weights = totals[g], []
            for i in range(count):
                s = scores[j + i, g]
                for half in range(2):
                    w = jnp.exp2(s[:, half * BLOCK : (half + 1) * BLOCK] * SCALE - peaks[g])
                    total = total + w
                    weights.append(w.astype(BF))
            totals[g] = total
            sums[g] += jnp.dot(
                jnp.concatenate(weights, axis=1), block_rows(values_ref, j, g, count), preferred_element_type=F32
            )

    def in_steps(total, step):
        pl.loop(0, total // 8)(lambda j: step(8 * j, 8))
        pl.when(total % 8 >= 4)(lambda: step(total // 8 * 8, 4))
        done = total // 4 * 4
        pl.when(total - done >= 2)(lambda: step(done, 2))
        pl.when(total % 2 == 1)(lambda: step(total - 1, 1))

    peaks[...] = jnp.full(peaks.shape, LOW_PEAK, F32)
    in_steps(pairs - 1, lambda j, count: score(j, count, False))
    score(pairs - 1, 1, True)

    for g in range(kv):
        peak = jnp.max(peaks[g], axis=1, keepdims=True) * SCALE
        peaks[g] = jnp.broadcast_to(peak.astype(BF).astype(F32), (rows, LANES))
    totals[...] = jnp.zeros(totals.shape, F32)
    sums[...] = jnp.zeros(sums.shape, F32)
    in_steps(pairs, accumulate)

    stats = [jnp.zeros((tokens, LANES), F32) for _ in range(n)]
    for g in range(kv):
        total = jnp.broadcast_to(jnp.sum(totals[g], axis=1, keepdims=True), (rows, LANES))
        coarse = total.astype(BF).astype(F32)
        for r in range(n):
            for a in range(group):
                h = g * group + a
                part = slice((r * group + a) * tokens, (r * group + a + 1) * tokens)
                message_refs[r][:, cols(h)] = sums[g, part].astype(BF)
                for at, value in enumerate((peaks[g, part], coarse[part], total[part] - coarse[part])):
                    stats[r] = jnp.where(stat_lane == 3 * h + at, value, stats[r])
    for r in range(n):
        message_refs[r][:, kv * group * HD :] = stats[r].astype(BF)


def attend(prepared, queries, after, kv):
    tokens, width = queries[0].shape
    n = len(queries)
    group = width // (kv * HD)
    keys, values, info = prepared
    slots = keys.shape[0] // BLOCK
    rows = n * group * tokens
    return pl.pallas_call(
        functools.partial(attend_body, (kv, group, tokens, n)),
        in_specs=[vmem_spec()] * (3 + n) + [pl.BlockSpec(memory_space=pl.ANY)],
        out_specs=[vmem_spec()] * n,
        out_shape=[jax.ShapeDtypeStruct((tokens, width + LANES), BF)] * n,
        scratch_shapes=[
            pltpu.VMEM(((slots + 1) // 2, kv, rows, 2 * BLOCK), F32),
            pltpu.VMEM((kv, rows, LANES), F32),
            pltpu.VMEM((kv, rows, LANES), F32),
            pltpu.VMEM((kv, rows, HD), F32),
        ],
        cost_estimate=pl.CostEstimate(flops=64 * 1024**2, bytes_accessed=0, transcendentals=0),
        compiler_params=params(),
        name="attend",
    )(info, keys, values, *queries, after)


def merge_body(heads, *refs):
    *parts, out_ref = refs
    loaded = [part[:, heads * HD :].astype(F32) for part in parts]
    for h in range(heads):
        peaks = [s[:, 3 * h : 3 * h + 1] for s in loaded]
        totals = [s[:, 3 * h + 1 : 3 * h + 2] + s[:, 3 * h + 2 : 3 * h + 3] for s in loaded]
        top = functools.reduce(jnp.maximum, peaks)
        factors = [jnp.exp2(p - top) for p in peaks]
        inverse = 1.0 / sum(f * t for f, t in zip(factors, totals, strict=True))
        cols = slice(h * HD, (h + 1) * HD)
        out_ref[:, cols] = sum(
            part[:, cols].astype(F32) * (f * inverse) for part, f in zip(parts, factors, strict=True)
        ).astype(BF)


def merge(parts, heads):
    tokens = parts[0].shape[0]
    return pl.pallas_call(
        functools.partial(merge_body, heads),
        in_specs=[pl.BlockSpec(memory_space=pltpu.VMEM)] * len(parts),
        out_specs=pl.BlockSpec(memory_space=pltpu.VMEM),
        out_shape=jax.ShapeDtypeStruct((tokens, heads * HD), BF),
        compiler_params=params(),
        name="merge",
    )(*parts)


def per_device(
    n_seq,
    n_head,
    segment_query,
    segment_memory,
    finished_memory,
    cache_memory,
    block_mask,
    owner_index,
    valid_count,
    output_weight,
):
    here = lax.axis_index("seq")
    own_tokens, width = segment_query.shape
    heads = width // HD
    kv = segment_memory.shape[2] // HD
    fin_blocks = finished_memory.shape[0] // BLOCK
    direct = n_seq == 4 and n_head == 4 and BLOCK == 2 * own_tokens

    def swap(value, axis, size, k):
        return lax.ppermute(value, axis, [(i, i ^ k) for i in range(size)])

    def gather_over_seq(value, between=lambda: None):
        near, far = swap(value, "seq", n_seq, 1), swap(value, "seq", n_seq, 2)
        made = between()
        if made is not None:
            far, made = lax.optimization_barrier((far, made))
        return [value, near, far, swap(far, "seq", n_seq, 1)], made

    if direct:
        shards = [(True, 2), (True, 0)]
        order = [2, 3, 1, 0]
    else:
        shards = [(False, i) for i in range(own_tokens * n_seq // BLOCK)]
    lists = make_lists(block_mask, owner_index, valid_count, "seq", own_tokens, shards, fin_blocks)

    def prepare_for(at, after):
        return prepare(at, lists, cache_memory, finished_memory, segment_memory, after)

    if direct:
        arrived, prepared = gather_over_seq(segment_query, lambda: prepare_for(0, []))
        batches = [[[arrived[k]] for k in order[:2]], [[arrived[k]] for k in order[2:]]]
    else:
        gathered = lax.all_gather(segment_query, "seq", axis=0, tiled=True)
        batches = [[[gathered[i * BLOCK : (i + 1) * BLOCK]]] for _, i in shards]
        prepared = prepare_for(0, [])

    messages, last = [], lists
    for at, of_block in enumerate(batches):
        prepared = prepared if at == 0 else prepare_for(at, [last] + of_block[0])
        for batch in of_block:
            messages += attend(prepared, batch, last, kv)
            last = messages[-1]

    if direct:
        parts = [m if k == 0 else swap(m, "seq", n_seq, k) for k, m in zip(order, messages, strict=True)]
        attended = merge([parts[i] for i in [3, 1, 0, 2]], heads)

        shards, _ = gather_over_seq(attended)
        head_at = lax.axis_index("head")
        core, side = head_at % 2, head_at // 2

        def project(rows):
            return jnp.dot(rows, output_weight, preferred_element_type=F32)

        def over_cores(pair):
            first_mine = (here ^ pair[0]) % 2 == core
            first, second = shards[pair[0]], shards[pair[1]]
            other = project(jnp.where(first_mine, second, first)).astype(BF)
            mine = project(jnp.where(first_mine, first, second))
            if pair[0] == 0:
                other, mine = lax.optimization_barrier((other, mine))
            received = swap(other, "head", n_head, 1)
            if pair[0] == 2:
                received, mine = lax.optimization_barrier((received, mine))
            return mine + received.astype(F32)

        near, far = over_cores((0, 1)), over_cores((2, 3))
        near_mine = here // 2 == side
        mine, other = jnp.where(near_mine, near, far), jnp.where(near_mine, far, near)
        return mine + swap(other.astype(BF), "head", n_head, 2).astype(F32)

    sent = jnp.concatenate(messages, axis=0)
    got = lax.all_to_all(sent, "seq", 0, 0, tiled=True).reshape(n_seq, own_tokens, -1)
    attended = merge([got[i] for i in range(n_seq)], heads)
    attended = lax.all_gather(attended, "seq", axis=0, tiled=True)
    return lax.psum_scatter(
        jnp.dot(attended, output_weight, preferred_element_type=F32), "head", scatter_dimension=0, tiled=True
    )


def solution(mesh):
    return jax.shard_map(
        functools.partial(per_device, mesh.shape["seq"], mesh.shape["head"]),
        mesh=mesh,
        in_specs=(
            P(("groups", "seq"), "head"),
            P(("groups", "seq"), None, "head"),
            P(("groups", "seq"), None, "head"),
            P(("groups", "seq"), None, "head"),
            P("groups", "seq"),
            P("groups"),
            P("groups"),
            P("head", "seq"),
        ),
        out_specs=P(("groups", "head"), "seq"),
        check_vma=False,
    )
```

```python
import functools
import math

import jax
import jax.numpy as jnp
from jax import lax
from jax.experimental import pallas as pl
from jax.experimental.pallas import tpu as pltpu
from jax.sharding import PartitionSpec as P

HD = 128
BLOCK = 128
LANES = 128
FLOOR = -1e30
LOW_PEAK = -1e29
SCALE = math.log2(math.e) / math.sqrt(HD)
BF = jnp.bfloat16
F32 = jnp.float32


VMEM_LIMIT = 26 << 20
UNROLL = 8


def params():
    return pltpu.CompilerParams(vmem_limit_bytes=VMEM_LIMIT)


def vmem_spec():
    return pl.BlockSpec(memory_space=pltpu.VMEM)


def smem_spec():
    return pl.BlockSpec(memory_space=pltpu.SMEM)


def list_body(axis, own_tokens, shards, fin_blocks, meta_ref, lists_ref):
    here = lax.axis_index(axis)
    ctx_blocks = meta_ref.shape[1]
    owner, valid = meta_ref[meta_ref.shape[0] - 2, 0], meta_ref[meta_ref.shape[0] - 1, 0]
    end = lists_ref.shape[1] - 3
    blocks = [((here ^ k) * own_tokens) // BLOCK if here_is_first else k for here_is_first, k in shards]

    def note(i, counts):
        for at, count in enumerate(counts):
            lists_ref[at, count] = i
        return tuple(
            count + jnp.where(meta_ref[block, i] > 0, 1, 0) for count, block in zip(counts, blocks, strict=True)
        )

    counts = lax.fori_loop(0, ctx_blocks, note, (jnp.int32(0),) * len(blocks))
    for at, count in enumerate(counts):
        for i in range(UNROLL - 1):
            lists_ref[at, count + i] = ctx_blocks - 1
        lists_ref[at, end] = count
        lists_ref[at, end + 1] = jnp.where(here == owner, 1, 0)
        lists_ref[at, end + 2] = jnp.clip(valid - here * own_tokens, 0, own_tokens)


def make_lists(mask, owner, count, axis, own_tokens, shards, fin_blocks):
    shape = (len(shards), mask.shape[1] + UNROLL + 3)
    rows = [jnp.pad(x[None], ((0, 0), (0, mask.shape[1] - 1))) for x in (owner, count)]
    meta = jnp.concatenate([mask] + rows)
    return pl.pallas_call(
        functools.partial(list_body, axis, own_tokens, shards, fin_blocks),
        in_specs=[smem_spec()],
        out_specs=smem_spec(),
        out_shape=jax.ShapeDtypeStruct(shape, jnp.int32),
        cost_estimate=pl.CostEstimate(flops=4 * 1024**3, bytes_accessed=0, transcendentals=0),
        compiler_params=params(),
        name="lists",
    )(meta)


def prepare_body(at, lists_ref, cache_ref, fin_ref, own_ref, *refs):
    keys_ref, values_ref, info_ref, list_ref, sem = refs[-5:]
    fetch = pltpu.make_async_copy(lists_ref, list_ref, sem)
    fetch.start()
    width = keys_ref.shape[1]
    row = lax.broadcasted_iota(jnp.int32, (2 * BLOCK, 2 * BLOCK), 0)
    col = lax.broadcasted_iota(jnp.int32, (2 * BLOCK, 2 * BLOCK), 1)
    source = jnp.where(row < BLOCK, 2 * row, 2 * row - 2 * BLOCK + 1)
    pick = jnp.where(col == source, 1.0, 0.0).astype(BF)

    def take_apart(pairs):
        parts = jnp.dot(pick, pairs.reshape(2 * BLOCK, width), preferred_element_type=F32).astype(BF)
        return parts[:BLOCK], parts[BLOCK:]

    def put(parts, to):
        rows = pl.ds(pl.multiple_of(to * BLOCK, BLOCK), BLOCK)
        keys_ref[rows], values_ref[rows] = parts

    fin_blocks, own_rows = fin_ref.shape[0] // BLOCK, own_ref.shape[0]
    filler = jnp.zeros((BLOCK - own_rows, 2, width), BF)
    own = take_apart(jnp.concatenate([own_ref[...], filler], axis=0))
    finished = [take_apart(fin_ref[i * BLOCK : (i + 1) * BLOCK]) for i in range(fin_blocks)]
    fetch.wait()
    end = list_ref.shape[1] - 3
    count, is_owner, limit = list_ref[at, end], list_ref[at, end + 1], list_ref[at, end + 2]
    full = count + is_owner * fin_blocks

    @pl.loop(0, (count + UNROLL - 1) // UNROLL)
    def _(j):
        for i in range(UNROLL):
            start = pl.multiple_of(list_ref[at, j * UNROLL + i] * BLOCK, BLOCK)
            put(take_apart(cache_ref[pl.ds(start, BLOCK)]), j * UNROLL + i)

    for i in range(fin_blocks):
        put(finished[i], count + i)
    put(own, full)
    zeros = jnp.zeros((BLOCK, width), BF)
    put((zeros, zeros), full + 1)

    pairs = (full + 2) // 2
    lane = lax.broadcasted_iota(jnp.int32, (8, 2 * BLOCK), 1)
    edge = jnp.where(full % 2 == 0, limit, BLOCK + limit)
    info_ref[:8] = jnp.zeros((8, 2 * BLOCK), F32) + pairs.astype(F32)
    info_ref[8:] = jnp.where(lane < edge, 0.0, FLOOR)


def prepare(at, lists, cache, finished, own, after):
    rows, _, width = cache.shape
    total = rows + finished.shape[0] + UNROLL * BLOCK
    return pl.pallas_call(
        functools.partial(prepare_body, at),
        in_specs=[vmem_spec()] * 4 + [pl.BlockSpec(memory_space=pl.ANY)] * len(after),
        out_specs=[vmem_spec()] * 3,
        out_shape=[jax.ShapeDtypeStruct((total, width), BF)] * 2 + [jax.ShapeDtypeStruct((16, 2 * BLOCK), F32)],
        scratch_shapes=[pltpu.SMEM(lists.shape, jnp.int32), pltpu.SemaphoreType.DMA],
        cost_estimate=pl.CostEstimate(flops=4 * 1024**3, bytes_accessed=12 * 1024**2, transcendentals=0),
        compiler_params=params(),
        name="prepare",
    )(lists, cache, finished, own, *after)


def attend_body(geometry, *refs):
    kv, group, tokens, n = geometry
    info_ref, keys_ref, values_ref = refs[:3]
    query_refs, message_refs = refs[3 : 3 + n], refs[4 + n : 4 + 2 * n]
    scores, peaks, totals, sums = refs[4 + 2 * n :]
    rows = n * group * tokens
    pairs = jnp.max(info_ref[:8, :LANES]).astype(jnp.int32)
    stat_lane = lax.broadcasted_iota(jnp.int32, (1, LANES), 1)

    def cols(h):
        return slice(h * HD, (h + 1) * HD)

    queries = [
        jnp.concatenate([ref[:, cols(g * group + a)] for ref in query_refs for a in range(group)], axis=0)
        for g in range(kv)
    ]

    def block_rows(ref, j, g, count):
        return ref[pl.ds(pl.multiple_of(2 * BLOCK * j, 2 * BLOCK), 2 * BLOCK * count), cols(g)]

    def score(j, count, masked):
        for g in range(kv):
            top = peaks[g]
            for i in range(count):
                s = lax.dot_general(
                    queries[g], block_rows(keys_ref, j + i, g, 1), (((1,), (1,)), ((), ())), preferred_element_type=F32
                )
                if masked:
                    s = s + info_ref[8:9]
                scores[j + i, g] = s
                top = jnp.maximum(top, jnp.maximum(s[:, :BLOCK], s[:, BLOCK:]))
            peaks[g] = top

    def accumulate(j, count):
        for g in range(kv):
            total, weights = totals[g], []
            for i in range(count):
                s = scores[j + i, g]
                for half in range(2):
                    w = jnp.exp2(s[:, half * BLOCK : (half + 1) * BLOCK] * SCALE - peaks[g])
                    total = total + w
                    weights.append(w.astype(BF))
            totals[g] = total
            sums[g] += jnp.dot(
                jnp.concatenate(weights, axis=1), block_rows(values_ref, j, g, count), preferred_element_type=F32
            )

    def in_steps(total, step):
        pl.loop(0, total // 8)(lambda j: step(8 * j, 8))
        pl.when(total % 8 >= 4)(lambda: step(total // 8 * 8, 4))
        done = total // 4 * 4
        pl.when(total - done >= 2)(lambda: step(done, 2))
        pl.when(total % 2 == 1)(lambda: step(total - 1, 1))

    peaks[...] = jnp.full(peaks.shape, LOW_PEAK, F32)
    in_steps(pairs - 1, lambda j, count: score(j, count, False))
    score(pairs - 1, 1, True)

    for g in range(kv):
        peak = jnp.max(peaks[g], axis=1, keepdims=True) * SCALE
        peaks[g] = jnp.broadcast_to(peak.astype(BF).astype(F32), (rows, LANES))
    totals[...] = jnp.zeros(totals.shape, F32)
    sums[...] = jnp.zeros(sums.shape, F32)
    in_steps(pairs, accumulate)

    stats = [jnp.zeros((tokens, LANES), F32) for _ in range(n)]
    for g in range(kv):
        total = jnp.broadcast_to(jnp.sum(totals[g], axis=1, keepdims=True), (rows, LANES))
        coarse = total.astype(BF).astype(F32)
        for r in range(n):
            for a in range(group):
                h = g * group + a
                part = slice((r * group + a) * tokens, (r * group + a + 1) * tokens)
                message_refs[r][:, cols(h)] = sums[g, part].astype(BF)
                for at, value in enumerate((peaks[g, part], coarse[part], total[part] - coarse[part])):
                    stats[r] = jnp.where(stat_lane == 3 * h + at, value, stats[r])
    for r in range(n):
        message_refs[r][:, kv * group * HD :] = stats[r].astype(BF)


def attend(prepared, queries, after, kv):
    tokens, width = queries[0].shape
    n = len(queries)
    group = width // (kv * HD)
    keys, values, info = prepared
    slots = keys.shape[0] // BLOCK
    rows = n * group * tokens
    return pl.pallas_call(
        functools.partial(attend_body, (kv, group, tokens, n)),
        in_specs=[vmem_spec()] * (3 + n) + [pl.BlockSpec(memory_space=pl.ANY)],
        out_specs=[vmem_spec()] * n,
        out_shape=[jax.ShapeDtypeStruct((tokens, width + LANES), BF)] * n,
        scratch_shapes=[
            pltpu.VMEM(((slots + 1) // 2, kv, rows, 2 * BLOCK), F32),
            pltpu.VMEM((kv, rows, LANES), F32),
            pltpu.VMEM((kv, rows, LANES), F32),
            pltpu.VMEM((kv, rows, HD), F32),
        ],
        cost_estimate=pl.CostEstimate(flops=64 * 1024**2, bytes_accessed=0, transcendentals=0),
        compiler_params=params(),
        name="attend",
    )(info, keys, values, *queries, after)


def merge_body(heads, *refs):
    *parts, out_ref = refs
    loaded = [part[:, heads * HD :].astype(F32) for part in parts]
    for h in range(heads):
        peaks = [s[:, 3 * h : 3 * h + 1] for s in loaded]
        totals = [s[:, 3 * h + 1 : 3 * h + 2] + s[:, 3 * h + 2 : 3 * h + 3] for s in loaded]
        top = functools.reduce(jnp.maximum, peaks)
        factors = [jnp.exp2(p - top) for p in peaks]
        inverse = 1.0 / sum(f * t for f, t in zip(factors, totals, strict=True))
        cols = slice(h * HD, (h + 1) * HD)
        out_ref[:, cols] = sum(
            part[:, cols].astype(F32) * (f * inverse) for part, f in zip(parts, factors, strict=True)
        ).astype(BF)


def merge(parts, heads):
    tokens = parts[0].shape[0]
    return pl.pallas_call(
        functools.partial(merge_body, heads),
        in_specs=[pl.BlockSpec(memory_space=pltpu.VMEM)] * len(parts),
        out_specs=pl.BlockSpec(memory_space=pltpu.VMEM),
        out_shape=jax.ShapeDtypeStruct((tokens, heads * HD), BF),
        compiler_params=params(),
        name="merge",
    )(*parts)


def per_device(
    n_seq,
    n_head,
    segment_query,
    segment_memory,
    finished_memory,
    cache_memory,
    block_mask,
    owner_index,
    valid_count,
    output_weight,
):
    here = lax.axis_index("seq")
    own_tokens, width = segment_query.shape
    heads = width // HD
    kv = segment_memory.shape[2] // HD
    fin_blocks = finished_memory.shape[0] // BLOCK
    direct = n_seq == 4 and n_head == 4 and BLOCK == 2 * own_tokens

    def swap(value, axis, size, k):
        return lax.ppermute(value, axis, [(i, i ^ k) for i in range(size)])

    def gather_over_seq(value, between=lambda: None):
        near, far = swap(value, "seq", n_seq, 1), swap(value, "seq", n_seq, 2)
        made = between()
        if made is not None:
            far, made = lax.optimization_barrier((far, made))
        return [value, near, far, swap(far, "seq", n_seq, 1)], made

    if direct:
        shards = [(True, 2), (True, 0)]
        order = [2, 3, 1, 0]
    else:
        shards = [(False, i) for i in range(own_tokens * n_seq // BLOCK)]
    lists = make_lists(block_mask, owner_index, valid_count, "seq", own_tokens, shards, fin_blocks)

    def prepare_for(at, after):
        return prepare(at, lists, cache_memory, finished_memory, segment_memory, after)

    if direct:
        arrived, prepared = gather_over_seq(segment_query, lambda: prepare_for(0, []))
        batches = [[[arrived[k]] for k in order[:2]], [[arrived[k]] for k in order[2:]]]
    else:
        gathered = lax.all_gather(segment_query, "seq", axis=0, tiled=True)
        batches = [[[gathered[i * BLOCK : (i + 1) * BLOCK]]] for _, i in shards]
        prepared = prepare_for(0, [])

    messages, last = [], lists
    for at, of_block in enumerate(batches):
        prepared = prepared if at == 0 else prepare_for(at, [last] + of_block[0])
        for batch in of_block:
            messages += attend(prepared, batch, last, kv)
            last = messages[-1]

    if direct:
        parts = [m if k == 0 else swap(m, "seq", n_seq, k) for k, m in zip(order, messages, strict=True)]
        attended = merge([parts[i] for i in [3, 1, 0, 2]], heads)

        shards, _ = gather_over_seq(attended)
        head_at = lax.axis_index("head")
        core, side = head_at % 2, head_at // 2

        def project(rows):
            return jnp.dot(rows, output_weight, preferred_element_type=F32)

        def over_cores(pair):
            first_mine = (here ^ pair[0]) % 2 == core
            first, second = shards[pair[0]], shards[pair[1]]
            other = project(jnp.where(first_mine, second, first)).astype(BF)
            mine = project(jnp.where(first_mine, first, second))
            if pair[0] == 0:
                other, mine = lax.optimization_barrier((other, mine))
            received = swap(other, "head", n_head, 1)
            if pair[0] == 2:
                received, mine = lax.optimization_barrier((received, mine))
            return mine + received.astype(F32)

        near, far = over_cores((0, 1)), over_cores((2, 3))
        near_mine = here // 2 == side
        mine, other = jnp.where(near_mine, near, far), jnp.where(near_mine, far, near)
        return mine + swap(other.astype(BF), "head", n_head, 2).astype(F32)

    sent = jnp.concatenate(messages, axis=0)
    got = lax.all_to_all(sent, "seq", 0, 0, tiled=True).reshape(n_seq, own_tokens, -1)
    attended = merge([got[i] for i in range(n_seq)], heads)
    attended = lax.all_gather(attended, "seq", axis=0, tiled=True)
    return lax.psum_scatter(
        jnp.dot(attended, output_weight, preferred_element_type=F32), "head", scatter_dimension=0, tiled=True
    )


def solution(mesh):
    return jax.shard_map(
        functools.partial(per_device, mesh.shape["seq"], mesh.shape["head"]),
        mesh=mesh,
        in_specs=(
            P(("groups", "seq"), "head"),
            P(("groups", "seq"), None, "head"),
            P(("groups", "seq"), None, "head"),
            P(("groups", "seq"), None, "head"),
            P("groups", "seq"),
            P("groups"),
            P("groups"),
            P("head", "seq"),
        ),
        out_specs=P(("groups", "head"), "seq"),
        check_vma=False,
    )
```
